32 devices in a mesh: dp: 4 (over z), tm: 2 (over x), head: 4 (over y, core).
Axes of the slice: x: 2, y: 2, z: 4, core: 2. Of those that a mesh axis runs over, the one named last changes fastest.
Arguments:
- frames: bfloat16 [4, 768, 1536], P('dp', 'tm')
- projections: bfloat16 [4, 1536, 1536], P(None, None, 'head')
- kernel: bfloat16 [32, 1536], replicated, may hold values from -1 to 1
- pattern: int32 [4, 12, 12], P('dp', 'tm'), may hold values from -1 to 11, as said below
- cotangent: bfloat16 [4, 768, 1536], P('dp', 'tm'), may hold values from -0.109375 to 0.109375
Outputs:
- encoded: bfloat16 [4, 768, 1536], P('dp', 'tm')
- proj_grad: float32 [4, 1536, 1536], P(None, ('dp', 'tm'), 'head')
- kernel_grad: float32 [32, 1536], P(('dp', 'tm'))
The draws below stay inside these ranges and needn't reach their ends.
Inputs may be any that keep to these rules, and one draw needn't show every extreme that they name: `pattern`: in each row the strided key blocks come first: phase + j * 1 for j = 0, 1, ..., one phase below 1 for the row, 1 to 12 of them; the remaining entries are -1.
All inputs are finite; a program needn't handle non-finite values.
Results may differ from the reference program's by a relative error of at most 0.04.
Values may be sent and summed in bfloat16 or wider, within the bound.
No kernel may reach another device: no remote copies, remote signals or barrier semaphores. Data moves between devices by JAX's collectives and lax.ppermute only.
A program may use at most 128 MiB of HBM per device.

```python
import jax
import jax.numpy as jnp
from jax import lax

D = 1536
HEADS = 16
HD = 96
BLK = 64
MAXSEL = 12
KW = 32
UTTS = 4
S = 768
NBLK = 12
STRIDE = 1


def draw_frames(key, part):
    subkeys = jax.random.split(key, 1)
    drawn = jnp.clip(jax.random.normal(subkeys[0], (UTTS, S, D), jnp.float32), -6.0, 6.0)
    return drawn.astype(jnp.bfloat16)


def draw_projections(key, part):
    drawn = jax.random.normal(key, (4, D, HEADS * HD), jnp.float32) * D ** (-0.5)
    return drawn.astype(jnp.bfloat16)


def draw_pattern(key, part):
    subkeys = jax.random.split(key, 3)
    blocks = jnp.arange(NBLK, dtype=jnp.int32)
    busy_start = jax.random.randint(subkeys[0], (UTTS, 1), 0, NBLK)
    busy_rows = (blocks[None, :] - busy_start) % NBLK < max(NBLK // 4, 1)
    entry_count = jnp.where(busy_rows, MAXSEL, jax.random.randint(subkeys[1], (UTTS, NBLK), 1, MAXSEL // 2 + 1))
    row_phase = jax.random.randint(subkeys[2], (UTTS, NBLK), 0, STRIDE)
    row_phase = jnp.where(blocks[None, :] == busy_start, STRIDE - 1, row_phase)
    slot_index = jnp.arange(MAXSEL, dtype=jnp.int32)
    entries = row_phase[:, :, None] + slot_index[None, None, :] * STRIDE
    return jnp.where(slot_index[None, None, :] < entry_count[:, :, None], entries, -1).astype(jnp.int32)


def block_levels(key, dims, shards, smallest, largest):
    factor_of, own = 1.0, jax.random.fold_in(key, 6)
    for dim, blocks in shards:
        steps = jnp.exp(jax.random.uniform(jax.random.fold_in(own, dim), (blocks,), jnp.float32, smallest / len(shards), largest / len(shards)))
        factor_of = factor_of * jnp.repeat(steps, dims[dim] // blocks).reshape([-1 if axis == dim else 1 for axis in range(len(dims))])
    return factor_of


def normal_values(stream_key, shape, deviation, reach, shards=(), held_as=jnp.bfloat16):
    level = block_levels(stream_key, shape, shards, -0.22, 0.18) if shards else 1.0
    values = jax.random.normal(stream_key, shape, jnp.float32) * deviation * level
    return jnp.minimum(jnp.maximum(values, -reach), reach).astype(held_as)


def setup_inputs(seed: int = 0) -> dict:
    splits = jax.random.split(jax.random.key(seed), 6)
    return {
        "frames": draw_frames(jax.random.fold_in(splits[5], 71), 0),
        "projections": draw_projections(jax.random.fold_in(splits[5], 71), 0),
        "kernel": normal_values(splits[2], (KW, D), KW ** -0.5, 1.0),
        "pattern": draw_pattern(jax.random.fold_in(splits[5], 71), 0),
        "cotangent": normal_values(splits[4], (UTTS, S, D), ((UTTS * S) ** -0.5), 0.109375, ((0, 4), (1, 2))),
    }


def key_lists(pattern, first_block, nblocks):
    query_count = pattern.shape[0]
    query_block = first_block + jnp.arange(query_count, dtype=jnp.int32)
    band_blocks = query_block[:, None] + jnp.arange(-1, 2, dtype=jnp.int32)[None, :]
    band_live = (band_blocks >= 0) & (band_blocks < nblocks)
    far_live = (pattern >= 0) & (jnp.abs(pattern - query_block[:, None]) > 1)
    listed = jnp.clip(jnp.concatenate([band_blocks, pattern], axis=1), 0, nblocks - 1).astype(jnp.int32)
    live_mask = jnp.concatenate([band_live, far_live], axis=1)
    return listed, live_mask


def gather_blocks(source, listed, block_len, head_dim):
    head_count = source.shape[1] // head_dim
    gathered = source.reshape(-1, block_len, head_count, head_dim)[listed]
    return gathered.reshape(listed.shape[0], listed.shape[1] * block_len, head_count, head_dim)


def masked_scores(query_tiles, key_tiles, live_mask, block_len):
    score_scale = query_tiles.shape[-1] ** -0.5
    scores = jnp.einsum("qthd,qkhd->qhtk", query_tiles.astype(jnp.float32), key_tiles.astype(jnp.float32)) * score_scale
    column_live = jnp.repeat(live_mask, block_len, axis=1)[:, None, None, :]
    return jnp.where(column_live, scores, -1e30), column_live


def attend(queries, key_rows, values, listed, live_mask, block_len, head_dim):
    head_count = queries.shape[1] // head_dim
    query_tiles = queries.reshape(listed.shape[0], block_len, head_count, head_dim)
    key_tiles = gather_blocks(key_rows, listed, block_len, head_dim)
    value_tiles = gather_blocks(values, listed, block_len, head_dim)
    scores, column_live = masked_scores(query_tiles, key_tiles, live_mask, block_len)
    highest = jnp.max(scores, axis=-1, keepdims=True)
    logsum = highest + jnp.log(jnp.sum(jnp.exp(scores - highest), axis=-1, keepdims=True))
    weights = jnp.where(column_live, jnp.exp(scores - logsum), 0.0).astype(jnp.bfloat16)
    mixed_rows = jnp.einsum("qhtk,qkhd->qthd", weights.astype(jnp.float32), value_tiles.astype(jnp.float32)).astype(jnp.bfloat16)
    return mixed_rows.reshape(queries.shape), logsum


def attend_back(queries, key_rows, values, listed, live_mask, logsum, mixed_rows, grad_mixed, block_len, head_dim, nblocks):
    head_count = queries.shape[1] // head_dim
    shape_tiles = (listed.shape[0], block_len, head_count, head_dim)
    query_tiles = queries.reshape(shape_tiles)
    grad_tiles = grad_mixed.reshape(shape_tiles).astype(jnp.float32)
    mixed_tiles = mixed_rows.reshape(shape_tiles).astype(jnp.float32)
    key_tiles = gather_blocks(key_rows, listed, block_len, head_dim)
    value_tiles = gather_blocks(values, listed, block_len, head_dim)
    scores, column_live = masked_scores(query_tiles, key_tiles, live_mask, block_len)
    probabilities = jnp.where(column_live, jnp.exp(scores - logsum), 0.0)
    weights = probabilities.astype(jnp.bfloat16)
    row_delta = jnp.einsum("qthd,qthd->qht", grad_tiles, mixed_tiles)
    grad_probs = jnp.einsum("qthd,qkhd->qhtk", grad_tiles, value_tiles.astype(jnp.float32))
    score_scale = head_dim ** -0.5
    grad_scores = (probabilities * (grad_probs - row_delta[..., None]) * score_scale).astype(jnp.bfloat16)
    grad_queries = jnp.einsum("qhtk,qkhd->qthd", grad_scores.astype(jnp.float32), key_tiles.astype(jnp.float32))
    grad_queries = grad_queries.astype(jnp.bfloat16).reshape(queries.shape)
    key_terms = jnp.einsum("qhtk,qthd->qkhd", grad_scores.astype(jnp.float32), query_tiles.astype(jnp.float32))
    value_terms = jnp.einsum("qhtk,qthd->qkhd", weights.astype(jnp.float32), grad_tiles)
    block_ids = jnp.arange(nblocks, dtype=jnp.int32)
    onehot = ((listed.reshape(-1)[:, None] == block_ids[None, :]) & live_mask.reshape(-1)[:, None]).astype(jnp.float32)
    tile_width = block_len * queries.shape[1]
    key_grad = jnp.dot(onehot.T, key_terms.reshape(-1, tile_width), precision=lax.Precision.HIGHEST)
    value_grad = jnp.dot(onehot.T, value_terms.reshape(-1, tile_width), precision=lax.Precision.HIGHEST)
    key_grad = key_grad.reshape(nblocks * block_len, queries.shape[1])
    value_grad = value_grad.reshape(nblocks * block_len, queries.shape[1])
    return grad_queries, key_grad, value_grad


def reference(frames, projections, kernel, pattern, cotangent):
    nblocks = S // BLK
    half_width = KW // 2
    contract = (((0,), (0,)), ((), ()))

    def one_utterance(inputs):
        source, rows_pattern, upstream = inputs
        listed, live_mask = key_lists(rows_pattern, 0, nblocks)
        queries = jnp.dot(source, projections[0], preferred_element_type=jnp.float32).astype(jnp.bfloat16)
        key_rows = jnp.dot(source, projections[1], preferred_element_type=jnp.float32).astype(jnp.bfloat16)
        values = jnp.dot(source, projections[2], preferred_element_type=jnp.float32).astype(jnp.bfloat16)
        mixed_rows, logsum = attend(queries, key_rows, values, listed, live_mask, BLK, HD)
        output_part = lax.dot_general(mixed_rows, projections[3], (((1,), (1,)), ((), ())), preferred_element_type=jnp.float32)
        residual = (source.astype(jnp.float32) + output_part).astype(jnp.bfloat16)
        padded = jnp.pad(residual, ((half_width, half_width), (0, 0)))
        padded_up = jnp.pad(upstream, ((half_width, half_width), (0, 0)))
        upstream_wide = upstream.astype(jnp.float32)
        encoded = residual.astype(jnp.float32)
        back_grad = upstream_wide
        taps_grad = []
        for offset in range(KW):
            weight_row = kernel[offset].astype(jnp.float32)
            shifted = padded[offset:offset + S].astype(jnp.float32)
            encoded = encoded + weight_row * shifted
            back_grad = back_grad + weight_row * padded_up[2 * half_width - offset:2 * half_width - offset + S].astype(jnp.float32)
            taps_grad.append(jnp.sum(upstream_wide * shifted, axis=0))
        encoded = encoded.astype(jnp.bfloat16)
        back_grad = back_grad.astype(jnp.bfloat16)
        kernel_grad = jnp.stack(taps_grad)
        grad_mixed = jnp.dot(back_grad, projections[3], preferred_element_type=jnp.float32).astype(jnp.bfloat16)
        grad_queries, key_grad, value_grad = attend_back(queries, key_rows, values, listed, live_mask, logsum, mixed_rows, grad_mixed, BLK, HD, nblocks)
        proj_grad = jnp.stack([
            lax.dot_general(source, grad_queries, contract, preferred_element_type=jnp.float32),
            lax.dot_general(source, key_grad.astype(jnp.bfloat16), contract, preferred_element_type=jnp.float32),
            lax.dot_general(source, value_grad.astype(jnp.bfloat16), contract, preferred_element_type=jnp.float32),
            lax.dot_general(back_grad, mixed_rows, contract, preferred_element_type=jnp.float32),
        ])
        return encoded, proj_grad, kernel_grad

    encoded, proj_grad, kernel_grad = lax.map(one_utterance, (frames, pattern, cotangent))
    return encoded, jnp.sum(proj_grad, axis=0), jnp.sum(kernel_grad, axis=0)
```

```python
import jax
import jax.numpy as jnp
from jax import lax
from jax.experimental import pallas as pl
from jax.experimental.pallas import tpu as pltpu
from jax.sharding import PartitionSpec as P

HD = 96
BLK = 64
KW = 32


def extended_2(array, sides, width):
    for axis, dim in sides:
        peers, length = (lax.axis_size(axis), array.shape[dim])
        up = [(i, (i + 1) % peers) for i in range(peers - 1)]
        down = [(j, i) for i, j in up]
        last = lax.slice_in_dim(array, length - width, length, axis=dim)
        first = lax.slice_in_dim(array, 0, width, axis=dim)
        before = lax.ppermute(last, axis, up)
        after = lax.ppermute(first, axis, down)
        array = jnp.concatenate([before, array, after], axis=dim)
    return array


def key_lists(pattern, first_block, nblocks):
    query_count = pattern.shape[0]
    query_block = first_block + jnp.arange(query_count, dtype=jnp.int32)
    band_blocks = query_block[:, None] + jnp.arange(-1, 2, dtype=jnp.int32)[None, :]
    band_live = (band_blocks >= 0) & (band_blocks < nblocks)
    far_live = (pattern >= 0) & (jnp.abs(pattern - query_block[:, None]) > 1)
    listed = jnp.clip(jnp.concatenate([band_blocks, pattern], axis=1), 0, nblocks - 1)
    live_mask = jnp.concatenate([band_live, far_live], axis=1)
    return (listed, live_mask)


def gather_blocks(source, listed, block_len, head_dim):
    head_count = source.shape[1] // head_dim
    gathered = source.reshape(-1, block_len, head_count, head_dim)[listed]
    return gathered.reshape(listed.shape[0], listed.shape[1] * block_len, head_count, head_dim)


def masked_scores(query_tiles, key_tiles, live_mask, block_len):
    score_scale = query_tiles.shape[-1] ** (-0.5)
    scores = (
        jnp.einsum("qthd,qkhd->qhtk", query_tiles, key_tiles, preferred_element_type=jnp.float32)
        * score_scale
    )
    column_live = jnp.repeat(live_mask, block_len, axis=1)[:, None, None, :]
    return (jnp.where(column_live, scores, -1e30), column_live)


def attend(queries, key_rows, values, listed, live_mask, block_len, head_dim):
    head_count = queries.shape[1] // head_dim
    query_tiles = queries.reshape(listed.shape[0], block_len, head_count, head_dim)
    key_tiles = gather_blocks(key_rows, listed, block_len, head_dim)
    value_tiles = gather_blocks(values, listed, block_len, head_dim)
    scores, column_live = masked_scores(query_tiles, key_tiles, live_mask, block_len)
    highest = jnp.max(scores, axis=-1, keepdims=True)
    logsum = highest + jnp.log(jnp.sum(jnp.exp(scores - highest), axis=-1, keepdims=True))
    weights = jnp.where(column_live, jnp.exp(scores - logsum), 0.0).astype(jnp.bfloat16)
    mixed_rows = jnp.einsum(
        "qhtk,qkhd->qthd", weights, value_tiles, preferred_element_type=jnp.float32
    ).astype(jnp.bfloat16)
    return (mixed_rows.reshape(queries.shape), logsum)


def attend_back(
    queries,
    key_rows,
    values,
    listed,
    live_mask,
    logsum,
    mixed_rows,
    grad_mixed,
    block_len,
    head_dim,
    nblocks,
):
    head_count = queries.shape[1] // head_dim
    shape_tiles = (listed.shape[0], block_len, head_count, head_dim)
    query_tiles = queries.reshape(shape_tiles)
    grad_tiles = grad_mixed.reshape(shape_tiles)
    mixed_tiles = mixed_rows.reshape(shape_tiles)
    key_tiles = gather_blocks(key_rows, listed, block_len, head_dim)
    value_tiles = gather_blocks(values, listed, block_len, head_dim)
    scores, column_live = masked_scores(query_tiles, key_tiles, live_mask, block_len)
    probabilities = jnp.where(column_live, jnp.exp(scores - logsum), 0.0)
    row_delta = jnp.einsum(
        "qthd,qthd->qht", grad_tiles, mixed_tiles, preferred_element_type=jnp.float32
    )
    grad_probs = jnp.einsum(
        "qthd,qkhd->qhtk", grad_tiles, value_tiles, preferred_element_type=jnp.float32
    )
    score_scale = head_dim ** (-0.5)
    grad_scores = (probabilities * (grad_probs - row_delta[..., None]) * score_scale).astype(
        jnp.bfloat16
    )
    grad_queries = jnp.einsum(
        "qhtk,qkhd->qthd", grad_scores, key_tiles, preferred_element_type=jnp.float32
    )
    grad_queries = grad_queries.astype(jnp.bfloat16).reshape(queries.shape)
    weights = probabilities.astype(jnp.bfloat16)
    key_terms = jnp.einsum(
        "qhtk,qthd->qkhd", grad_scores, query_tiles, preferred_element_type=jnp.float32
    )
    value_terms = jnp.einsum(
        "qhtk,qthd->qkhd", weights, grad_tiles, preferred_element_type=jnp.float32
    )
    block_ids = jnp.arange(nblocks, dtype=jnp.int32)
    onehot = (
        (listed.reshape(-1)[:, None] == block_ids[None, :]) & live_mask.reshape(-1)[:, None]
    ).astype(jnp.float32)
    tile_width = block_len * queries.shape[1]
    key_grad = jnp.dot(onehot.T, key_terms.reshape(-1, tile_width), precision=lax.Precision.HIGHEST)
    value_grad = jnp.dot(
        onehot.T, value_terms.reshape(-1, tile_width), precision=lax.Precision.HIGHEST
    )
    key_grad = key_grad.reshape(nblocks * block_len, queries.shape[1])
    value_grad = value_grad.reshape(nblocks * block_len, queries.shape[1])
    return (grad_queries, row_delta, key_grad, value_grad)


def conv_apply(residual, upstream, extended, kernel_cols, frame_count, width, half_width):
    padded = extended[:, :width]
    padded_up = extended[:, width:]
    upstream_wide = upstream.astype(jnp.float32)
    encoded = residual.astype(jnp.float32)
    back_grad = upstream_wide
    taps_grad = []
    for offset in range(2 * half_width):
        weight_row = kernel_cols[offset].astype(jnp.float32)
        shifted = padded[offset : offset + frame_count].astype(jnp.float32)
        encoded = encoded + weight_row * shifted
        back_grad = back_grad + weight_row * padded_up[
            2 * half_width - offset : 2 * half_width - offset + frame_count
        ].astype(jnp.float32)
        taps_grad.append(jnp.sum(upstream_wide * shifted, axis=0))
    return (encoded.astype(jnp.bfloat16), back_grad.astype(jnp.bfloat16), jnp.stack(taps_grad))


def shards(frames, projections, kernel, pattern, cotangent):
    source = frames[0]
    upstream = cotangent[0]
    rows_pattern = pattern[0]
    frame_count = source.shape[0]
    model_width = source.shape[1]
    head_width = projections.shape[2]
    local_blocks = frame_count // BLK
    cycle_size = lax.axis_size("tm")
    nblocks = local_blocks * cycle_size
    first_block = lax.axis_index("tm") * local_blocks
    half_width = KW // 2
    contract = (((0,), (0,)), ((), ()))
    listed, live_mask = key_lists(rows_pattern, first_block, nblocks)
    queries = jnp.dot(source, projections[0], preferred_element_type=jnp.float32).astype(
        jnp.bfloat16
    )
    key_rows = jnp.dot(source, projections[1], preferred_element_type=jnp.float32).astype(
        jnp.bfloat16
    )
    values = jnp.dot(source, projections[2], preferred_element_type=jnp.float32).astype(
        jnp.bfloat16
    )
    key_all, value_all = (
        lax.all_gather(key_rows, "tm", axis=0, tiled=True),
        lax.all_gather(values, "tm", axis=0, tiled=True),
    )
    mixed_rows, logsum = attend(queries, key_all, value_all, listed, live_mask, BLK, HD)
    output_part = lax.dot_general(
        mixed_rows, projections[3], (((1,), (1,)), ((), ())), preferred_element_type=jnp.float32
    )
    summed = lax.psum(output_part.astype(jnp.bfloat16), "head").astype(jnp.float32)
    residual = (source.astype(jnp.float32) + summed).astype(jnp.bfloat16)
    extended = extended_2(jnp.concatenate([residual, upstream], axis=1), (("tm", 0),), half_width)
    encoded, back_grad, kernel_grad = conv_apply(
        residual, upstream, extended, kernel, frame_count, model_width, half_width
    )
    grad_mixed = jnp.dot(back_grad, projections[3], preferred_element_type=jnp.float32).astype(
        jnp.bfloat16
    )
    grad_queries, row_delta, key_grad, value_grad = attend_back(
        queries,
        key_all,
        value_all,
        listed,
        live_mask,
        logsum,
        mixed_rows,
        grad_mixed,
        BLK,
        HD,
        nblocks,
    )
    key_value_terms = jnp.concatenate([key_grad, value_grad], axis=1)
    owned = lax.psum_scatter(
        key_value_terms.astype(jnp.bfloat16), "tm", scatter_dimension=0, tiled=True
    ).astype(jnp.float32)
    key_own = owned[:, :head_width].astype(jnp.bfloat16)
    value_own = owned[:, head_width:].astype(jnp.bfloat16)
    proj_grad = jnp.stack(
        [
            lax.dot_general(source, grad_queries, contract, preferred_element_type=jnp.float32),
            lax.dot_general(source, key_own, contract, preferred_element_type=jnp.float32),
            lax.dot_general(source, value_own, contract, preferred_element_type=jnp.float32),
            lax.dot_general(back_grad, mixed_rows, contract, preferred_element_type=jnp.float32),
        ]
    )
    proj_result, kernel_result = (
        lax.psum_scatter(
            proj_grad.astype(jnp.bfloat16), ("dp", "tm"), scatter_dimension=1, tiled=True
        ).astype(jnp.float32),
        lax.psum_scatter(
            kernel_grad.astype(jnp.bfloat16), ("dp", "tm"), scatter_dimension=0, tiled=True
        ).astype(jnp.float32),
    )
    return (encoded[None], proj_result, kernel_result)


def attention_kernel(bias_ref, qkv_own, qkv_far, grad_own, grad_far, mixed_own, mixed_far, terms_own, terms_far):
    half = qkv_own.shape[0]
    width = grad_own.shape[1]
    scale = HD ** (-0.5)
    nn = (((1,), (0,)), ((), ()))
    nt = (((1,), (1,)), ((), ()))
    tn = (((0,), (0,)), ((), ()))
    f32 = jnp.float32

    def dot(a, b, dims):
        return lax.dot_general(a, b, dims, preferred_element_type=f32)

    for head in range(width // HD):
        cols = slice(head * HD, (head + 1) * HD)
        kcols = slice(width + head * HD, width + (head + 1) * HD)
        vcols = slice(2 * width + head * HD, 2 * width + (head + 1) * HD)
        keys = jnp.concatenate([qkv_own[:, kcols], qkv_far[:, kcols]], axis=0)
        vals = jnp.concatenate([qkv_own[:, vcols], qkv_far[:, vcols]], axis=0)
        key_grad = jnp.zeros((2 * half, HD), f32)
        value_grad = jnp.zeros((2 * half, HD), f32)
        for part in range(2):
            qkv, grads = (qkv_own, grad_own) if part == 0 else (qkv_far, grad_far)
            mixed_out, terms = (mixed_own, terms_own) if part == 0 else (mixed_far, terms_far)
            query = qkv[:, cols]
            grad = grads[:, cols]
            bias = bias_ref[:, part * half : (part + 1) * half]
            blocks = bias.shape[0]
            bias = jnp.broadcast_to(bias[:, None, :], (blocks, BLK, half)).reshape(blocks * BLK, half)
            scores = dot(keys, query, nt) * scale + bias
            highest = jnp.max(scores, axis=0, keepdims=True)
            powers = jnp.exp(scores - highest)
            prob = powers * (1.0 / jnp.sum(powers, axis=0, keepdims=True))
            weights = prob.astype(jnp.bfloat16)
            mixed_t = dot(vals, weights, tn).astype(jnp.bfloat16)
            delta = jnp.sum(grad.T.astype(f32) * mixed_t.astype(f32), axis=0, keepdims=True)
            grad_prob = dot(vals, grad, nt)
            grad_scores = (prob * (grad_prob - delta) * scale).astype(jnp.bfloat16)
            mixed_out[:, cols] = mixed_t.T
            terms[:, cols] = dot(keys, grad_scores, tn).T.astype(jnp.bfloat16)
            key_grad = key_grad + dot(grad_scores, query, nn)
            value_grad = value_grad + dot(weights, grad, nn)
        for part in range(2):
            terms = terms_own if part == 0 else terms_far
            rows = slice(part * half, (part + 1) * half)
            terms[:, kcols] = key_grad[rows].astype(jnp.bfloat16)
            terms[:, vcols] = value_grad[rows].astype(jnp.bfloat16)


def attention(bias, qkv_own, qkv_far, grad_own, grad_far):
    half, width = grad_own.shape
    mixed = jax.ShapeDtypeStruct((half, width), jnp.bfloat16)
    terms = jax.ShapeDtypeStruct((half, 3 * width), jnp.bfloat16)
    pairs = (2 * half) ** 2 * (width // HD)
    return pl.pallas_call(
        attention_kernel,
        out_shape=(mixed, mixed, terms, terms),
        compiler_params=pltpu.CompilerParams(vmem_limit_bytes=48 << 20),
        cost_estimate=pl.CostEstimate(
            flops=14 * pairs * HD, bytes_accessed=12 * half * width * 2, transcendentals=pairs
        ),
        name="attention",
    )(bias, qkv_own, qkv_far, grad_own, grad_far)


LANES = 128


def conv_rows(rows):
    return next(size for size in (64, 48, 32, 16) if rows % size == 0)


def fill_padded(padded, rows_ref, halo_ref, flag_ref, cols):
    half_width = KW // 2
    count = rows_ref.shape[0]
    halo = halo_ref[:, cols].astype(jnp.float32)
    upper = flag_ref[0, 0] == 1
    padded[0:half_width] = jnp.where(upper, halo, 0.0)
    padded[half_width : half_width + count] = rows_ref[:, cols].astype(jnp.float32)
    padded[half_width + count : 2 * half_width + count] = jnp.where(upper, 0.0, halo)


def back_conv_kernel(flag_ref, up_ref, halo_ref, taps_ref, out_ref, padded):
    count = up_ref.shape[0]
    step = conv_rows(count)
    for chunk in range(up_ref.shape[1] // LANES):
        cols = slice(chunk * LANES, (chunk + 1) * LANES)
        fill_padded(padded, up_ref, halo_ref, flag_ref, cols)
        taps = taps_ref[:, cols].astype(jnp.float32)

        def body(tile, carry, cols=cols, taps=taps):
            start = pl.multiple_of(tile * step, step)
            total = padded[pl.ds(start + KW // 2, step)]
            for offset in range(KW):
                total = total + taps[offset : offset + 1] * padded[pl.ds(start + KW - offset, step)]
            out_ref[pl.ds(start, step), cols] = total.astype(jnp.bfloat16)
            return carry

        lax.fori_loop(0, count // step, body, 0)


def back_conv(flag, upstream, halo, taps):
    count, width = upstream.shape
    return pl.pallas_call(
        back_conv_kernel,
        out_shape=jax.ShapeDtypeStruct((count, width), jnp.bfloat16),
        in_specs=[pl.BlockSpec(memory_space=pltpu.SMEM)] + [pl.BlockSpec(memory_space=pltpu.VMEM)] * 3,
        scratch_shapes=[pltpu.VMEM((count + KW + 8, LANES), jnp.float32)],
        cost_estimate=pl.CostEstimate(flops=2 * KW * count * width * 40, bytes_accessed=4 * count * width, transcendentals=0),
        name="back_conv",
    )(flag, upstream, halo, taps)


def conv_kernel(flag_ref, rows_ref, halo_ref, up_ref, taps_ref, out_ref, grad_ref, padded, sums):
    count = rows_ref.shape[0]
    step = conv_rows(count)
    for chunk in range(rows_ref.shape[1] // LANES):
        cols = slice(chunk * LANES, (chunk + 1) * LANES)
        fill_padded(padded, rows_ref, halo_ref, flag_ref, cols)
        taps = taps_ref[:, cols].astype(jnp.float32)
        sums[...] = jnp.zeros_like(sums)

        def body(tile, carry, cols=cols, taps=taps):
            start = pl.multiple_of(tile * step, step)
            total = padded[pl.ds(start + KW // 2, step)]
            upstream = up_ref[pl.ds(start, step), cols].astype(jnp.float32)
            for offset in range(KW):
                shifted = padded[pl.ds(start + offset, step)]
                total = total + taps[offset : offset + 1] * shifted
                product = (upstream * shifted).reshape(step // 8, 8, LANES)
                sums[offset] = sums[offset] + jnp.sum(product, axis=0)
            out_ref[pl.ds(start, step), cols] = total.astype(jnp.bfloat16)
            return carry

        lax.fori_loop(0, count // step, body, 0)
        grad_ref[:, cols] = jnp.sum(sums[...], axis=1)


def conv(flag, rows, halo, upstream, taps):
    count, width = rows.shape
    return pl.pallas_call(
        conv_kernel,
        out_shape=(
            jax.ShapeDtypeStruct((count, width), jnp.bfloat16),
            jax.ShapeDtypeStruct((KW, width), jnp.float32),
        ),
        in_specs=[pl.BlockSpec(memory_space=pltpu.SMEM)] + [pl.BlockSpec(memory_space=pltpu.VMEM)] * 4,
        scratch_shapes=[
            pltpu.VMEM((count + KW + 8, LANES), jnp.float32),
            pltpu.VMEM((KW, 8, LANES), jnp.float32),
        ],
        cost_estimate=pl.CostEstimate(flops=4 * KW * count * width * 40, bytes_accessed=6 * count * width, transcendentals=0),
        name="conv",
    )(flag, rows, halo, upstream, taps)


SIDE = [(0, 1), (1, 0)]
CORE = [(0, 1), (1, 0), (2, 3), (3, 2)]
CHIP = [(0, 2), (2, 0), (1, 3), (3, 1)]


def columns(array, index, width):
    return lax.dynamic_slice_in_dim(array, index * width, width, axis=1)


def far_quarters(array, head, width):
    mine = lax.ppermute(columns(array, head, width), "tm", SIDE)
    beside = lax.ppermute(mine, "head", CHIP)
    pair = jnp.stack([mine, beside])
    other = lax.ppermute(pair, "head", CORE)
    return jnp.stack([mine, other[0], beside, other[1]])


def live_bias(pattern, far_pattern, side, local):
    order = jnp.concatenate(
        [side * local + jnp.arange(local), (1 - side) * local + jnp.arange(local)]
    ).astype(jnp.int32)
    chosen = jnp.concatenate([pattern, far_pattern], axis=0)
    near = jnp.abs(order[:, None] - order[None, :]) <= 1
    listed = jnp.any(chosen[None, :, :] == order[:, None, None], axis=-1)
    bias = jnp.where(near | listed, 0.0, -1e30).astype(jnp.float32)
    return jnp.repeat(bias, BLK, axis=1)


def split_heads(frames, projections, kernel, pattern, cotangent):
    bf16, f32 = (jnp.bfloat16, jnp.float32)
    source, upstream = (frames[0], cotangent[0])
    count, width = source.shape
    local = count // BLK
    half_width = KW // 2
    ring_size = lax.axis_size("dp")
    head_width = projections.shape[2]
    mine_width = head_width // 2
    quarter = width // 4
    shard = width // ring_size
    side, head, place = (lax.axis_index("tm"), lax.axis_index("head"), lax.axis_index("dp"))
    first = side == 0
    flag = side.astype(jnp.int32).reshape(1, 1)
    tn = (((0,), (0,)), ((), ()))

    def pick(array):
        low, high = (array[:, :mine_width], array[:, mine_width:])
        return (jnp.where(first, low, high), jnp.where(first, high, low))

    def edge(array):
        return jnp.where(first, array[count - half_width :], array[:half_width])

    far_pattern = lax.ppermute(pattern[0], "tm", SIDE)
    up_halo = lax.ppermute(edge(upstream), "tm", SIDE)
    keeps, sends = ([], [])
    for index in range(3):
        whole = jnp.dot(source, projections[index], preferred_element_type=f32).astype(bf16)
        keep, send = pick(whole)
        keeps.append(keep)
        sends.append(send)
    qkv_own = jnp.concatenate(keeps, axis=1)
    qkv_send = jnp.concatenate(sends, axis=1)
    qkv_far = lax.ppermute(qkv_send, "tm", SIDE)
    bias = live_bias(pattern[0], far_pattern, side, local)

    back_grad = back_conv(flag, upstream, up_halo, kernel)
    grad_mixed = jnp.dot(back_grad, projections[3], preferred_element_type=f32).astype(bf16)
    grad_own, grad_send = pick(grad_mixed)
    grad_far = lax.ppermute(grad_send, "tm", SIDE)
    late_source, _ = lax.optimization_barrier((source, qkv_send))
    far_frames = far_quarters(late_source, head, quarter)
    far_back = far_quarters(back_grad, head, quarter)

    mixed_own, mixed_far, terms_own, terms_far = attention(bias, qkv_own, qkv_far, grad_own, grad_far)

    mixed_back = lax.ppermute(mixed_far, "tm", SIDE)
    mixed_rows = jnp.concatenate(
        [jnp.where(first, mixed_own, mixed_back), jnp.where(first, mixed_back, mixed_own)], axis=1
    )

    def step_chunk(step):
        index = (place + (2 * ring_size - 1 - step)) % ring_size
        piece = index ^ head
        far_f = lax.dynamic_index_in_dim(far_frames, piece, 0, keepdims=False)
        far_b = lax.dynamic_index_in_dim(far_back, piece, 0, keepdims=False)
        near_f = columns(source, index, shard)
        near_b = columns(back_grad, index, shard)
        attn = lax.dot_general(near_f, terms_own, tn, preferred_element_type=f32) + lax.dot_general(
            far_f, terms_far, tn, preferred_element_type=f32
        )
        out = lax.dot_general(near_b, mixed_own, tn, preferred_element_type=f32) + lax.dot_general(
            far_b, mixed_far, tn, preferred_element_type=f32
        )
        return jnp.concatenate([attn, out], axis=1)

    onward = [(i, (i + 1) % ring_size) for i in range(ring_size)]
    chunk = step_chunk(0).astype(bf16)
    for step in range(1, ring_size):
        arrived = lax.ppermute(chunk, "dp", onward)
        chunk = (step_chunk(step) + arrived.astype(f32)).astype(bf16)

    output_part = lax.dot_general(
        mixed_rows, projections[3], (((1,), (1,)), ((), ())), preferred_element_type=f32
    ).astype(bf16)
    low_core = head % 2 == 0
    low_chip = head // 2 == 0
    parts = [output_part[:, i * quarter : (i + 1) * quarter] for i in range(4)]
    core_keep = [jnp.where(low_core, parts[2 * i], parts[2 * i + 1]) for i in range(2)]
    core_send = jnp.stack([jnp.where(low_core, parts[2 * i + 1], parts[2 * i]) for i in range(2)])
    core_got = lax.ppermute(core_send, "head", CORE)
    chip_sum = [core_keep[i].astype(f32) + core_got[i].astype(f32) for i in range(2)]
    chip_send = jnp.where(low_chip, chip_sum[1], chip_sum[0]).astype(bf16)
    chip_got = lax.ppermute(chip_send, "head", CHIP)
    summed = jnp.where(low_chip, chip_sum[0], chip_sum[1]) + chip_got.astype(f32)
    residual = (columns(source, head, quarter).astype(f32) + summed).astype(bf16)
    res_halo = lax.ppermute(edge(residual), "tm", SIDE)
    encoded, taps_grad = conv(
        flag, residual, res_halo, columns(upstream, head, quarter), columns(kernel, head, quarter)
    )

    beside = lax.ppermute(encoded, "head", CHIP)
    pair = jnp.stack([encoded, beside])
    other = lax.ppermute(pair, "head", CORE)
    pieces = [encoded, other[0], beside, other[1]]
    encoded_all = jnp.concatenate(
        [lax.select_n((head ^ i).astype(jnp.int32), *pieces) for i in range(4)], axis=1
    )

    tap_rows = KW // (2 * ring_size)
    grouped = taps_grad.reshape(ring_size, 2, tap_rows, quarter)
    tap_keep = jnp.where(first, grouped[:, 0], grouped[:, 1])
    tap_send = jnp.where(first, grouped[:, 1], grouped[:, 0])
    tap_sum = tap_keep + lax.ppermute(tap_send, "tm", SIDE)
    tap_total = lax.dynamic_index_in_dim(tap_sum, place, 0, keepdims=False)
    for hop in range(1, ring_size):
        target = (place + hop) % ring_size
        leaving = lax.dynamic_index_in_dim(tap_sum, target, 0, keepdims=False)
        tap_total = tap_total + lax.ppermute(
            leaving, "dp", [(i, (i + hop) % ring_size) for i in range(ring_size)]
        )
    tap_beside = lax.ppermute(tap_total, "head", CHIP)
    tap_other = lax.ppermute(jnp.stack([tap_total, tap_beside]), "head", CORE)
    tap_pieces = [tap_total, tap_other[0], tap_beside, tap_other[1]]
    kernel_result = jnp.concatenate(
        [lax.select_n((head ^ i).astype(jnp.int32), *tap_pieces) for i in range(4)], axis=1
    )

    rows = shard // 2
    final_keep = jnp.where(first, chunk[:rows], chunk[rows:])
    final_send = jnp.where(first, chunk[rows:], chunk[:rows])
    final_got = lax.ppermute(final_send, "tm", SIDE)
    left = jnp.where(first, final_keep, final_got)
    right = jnp.where(first, final_got, final_keep)
    proj_result = jnp.stack(
        [
            jnp.concatenate(
                [x[:, i * mine_width : (i + 1) * mine_width] for x in (left, right)], axis=1
            )
            for i in range(4)
        ]
    ).astype(f32)
    return (encoded_all[None], proj_result, kernel_result)


def solution(mesh):
    placed = (
        P("dp", "tm", None),
        P(None, None, "head"),
        P(),
        P("dp", "tm", None),
        P("dp", "tm", None),
    )
    sizes = dict(mesh.shape)

    def chosen(frames, projections, kernel, pattern, cotangent):
        fits = (
            sizes["tm"] == 2
            and sizes["head"] == 4
            and sizes["dp"] == 4
            and frames.shape[1] <= 768
            and projections.shape[2] // 4 == 4 * HD
            and frames.shape[2] % (4 * LANES) == 0
        )
        body = split_heads if fits else shards
        return jax.shard_map(
            body,
            mesh=mesh,
            in_specs=placed,
            out_specs=(P("dp", "tm", None), P(None, ("dp", "tm"), "head"), P(("dp", "tm"), None)),
            check_vma=False,
        )(frames, projections, kernel, pattern, cotangent)

    return chosen
```

```python
import jax
import jax.numpy as jnp
from jax import lax
from jax.experimental import pallas as pl
from jax.experimental.pallas import tpu as pltpu
from jax.sharding import PartitionSpec as P


HD = 96
BLK = 64
KW = 32


def extended_2(array, sides, width):
    for axis, dim in sides:
        peers, length = (lax.axis_size(axis), array.shape[dim])
        up = [(i, (i + 1) % peers) for i in range(peers - 1)]
        down = [(j, i) for i, j in up]
        last = lax.slice_in_dim(array, length - width, length, axis=dim)
        first = lax.slice_in_dim(array, 0, width, axis=dim)
        before = lax.ppermute(last, axis, up)
        after = lax.ppermute(first, axis, down)
        array = jnp.concatenate([before, array, after], axis=dim)
    return array


def key_lists(pattern, first_block, nblocks):
    query_count = pattern.shape[0]
    query_block = first_block + jnp.arange(query_count, dtype=jnp.int32)
    band_blocks = query_block[:, None] + jnp.arange(-1, 2, dtype=jnp.int32)[None, :]
    band_live = (band_blocks >= 0) & (band_blocks < nblocks)
    far_live = (pattern >= 0) & (jnp.abs(pattern - query_block[:, None]) > 1)
    listed = jnp.clip(jnp.concatenate([band_blocks, pattern], axis=1), 0, nblocks - 1)
    live_mask = jnp.concatenate([band_live, far_live], axis=1)
    return (listed, live_mask)


def gather_blocks(source, listed, block_len, head_dim):
    head_count = source.shape[1] // head_dim
    gathered = source.reshape(-1, block_len, head_count, head_dim)[listed]
    return gathered.reshape(listed.shape[0], listed.shape[1] * block_len, head_count, head_dim)


def masked_scores(query_tiles, key_tiles, live_mask, block_len):
    score_scale = query_tiles.shape[-1] ** (-0.5)
    scores = (
        jnp.einsum("qthd,qkhd->qhtk", query_tiles, key_tiles, preferred_element_type=jnp.float32)
        * score_scale
    )
    column_live = jnp.repeat(live_mask, block_len, axis=1)[:, None, None, :]
    return (jnp.where(column_live, scores, -1e30), column_live)


def attend(queries, key_rows, values, listed, live_mask, block_len, head_dim):
    head_count = queries.shape[1] // head_dim
    query_tiles = queries.reshape(listed.shape[0], block_len, head_count, head_dim)
    key_tiles = gather_blocks(key_rows, listed, block_len, head_dim)
    value_tiles = gather_blocks(values, listed, block_len, head_dim)
    scores, column_live = masked_scores(query_tiles, key_tiles, live_mask, block_len)
    highest = jnp.max(scores, axis=-1, keepdims=True)
    logsum = highest + jnp.log(jnp.sum(jnp.exp(scores - highest), axis=-1, keepdims=True))
    weights = jnp.where(column_live, jnp.exp(scores - logsum), 0.0).astype(jnp.bfloat16)
    mixed_rows = jnp.einsum(
        "qhtk,qkhd->qthd", weights, value_tiles, preferred_element_type=jnp.float32
    ).astype(jnp.bfloat16)
    return (mixed_rows.reshape(queries.shape), logsum)


def attend_back(
    queries,
    key_rows,
    values,
    listed,
    live_mask,
    logsum,
    mixed_rows,
    grad_mixed,
    block_len,
    head_dim,
    nblocks,
):
    head_count = queries.shape[1] // head_dim
    shape_tiles = (listed.shape[0], block_len, head_count, head_dim)
    query_tiles = queries.reshape(shape_tiles)
    grad_tiles = grad_mixed.reshape(shape_tiles)
    mixed_tiles = mixed_rows.reshape(shape_tiles)
    key_tiles = gather_blocks(key_rows, listed, block_len, head_dim)
    value_tiles = gather_blocks(values, listed, block_len, head_dim)
    scores, column_live = masked_scores(query_tiles, key_tiles, live_mask, block_len)
    probabilities = jnp.where(column_live, jnp.exp(scores - logsum), 0.0)
    row_delta = jnp.einsum(
        "qthd,qthd->qht", grad_tiles, mixed_tiles, preferred_element_type=jnp.float32
    )
    grad_probs = jnp.einsum(
        "qthd,qkhd->qhtk", grad_tiles, value_tiles, preferred_element_type=jnp.float32
    )
    score_scale = head_dim ** (-0.5)
    grad_scores = (probabilities * (grad_probs - row_delta[..., None]) * score_scale).astype(
        jnp.bfloat16
    )
    grad_queries = jnp.einsum(
        "qhtk,qkhd->qthd", grad_scores, key_tiles, preferred_element_type=jnp.float32
    )
    grad_queries = grad_queries.astype(jnp.bfloat16).reshape(queries.shape)
    weights = probabilities.astype(jnp.bfloat16)
    key_terms = jnp.einsum(
        "qhtk,qthd->qkhd", grad_scores, query_tiles, preferred_element_type=jnp.float32
    )
    value_terms = jnp.einsum(
        "qhtk,qthd->qkhd", weights, grad_tiles, preferred_element_type=jnp.float32
    )
    block_ids = jnp.arange(nblocks, dtype=jnp.int32)
    onehot = (
        (listed.reshape(-1)[:, None] == block_ids[None, :]) & live_mask.reshape(-1)[:, None]
    ).astype(jnp.float32)
    tile_width = block_len * queries.shape[1]
    key_grad = jnp.dot(onehot.T, key_terms.reshape(-1, tile_width), precision=lax.Precision.HIGHEST)
    value_grad = jnp.dot(
        onehot.T, value_terms.reshape(-1, tile_width), precision=lax.Precision.HIGHEST
    )
    key_grad = key_grad.reshape(nblocks * block_len, queries.shape[1])
    value_grad = value_grad.reshape(nblocks * block_len, queries.shape[1])
    return (grad_queries, row_delta, key_grad, value_grad)


def conv_apply(residual, upstream, extended, kernel_cols, frame_count, width, half_width):
    padded = extended[:, :width]
    padded_up = extended[:, width:]
    upstream_wide = upstream.astype(jnp.float32)
    encoded = residual.astype(jnp.float32)
    back_grad = upstream_wide
    taps_grad = []
    for offset in range(2 * half_width):
        weight_row = kernel_cols[offset].astype(jnp.float32)
        shifted = padded[offset : offset + frame_count].astype(jnp.float32)
        encoded = encoded + weight_row * shifted
        back_grad = back_grad + weight_row * padded_up[
            2 * half_width - offset : 2 * half_width - offset + frame_count
        ].astype(jnp.float32)
        taps_grad.append(jnp.sum(upstream_wide * shifted, axis=0))
    return (encoded.astype(jnp.bfloat16), back_grad.astype(jnp.bfloat16), jnp.stack(taps_grad))


def shards(frames, projections, kernel, pattern, cotangent):
    source = frames[0]
    upstream = cotangent[0]
    rows_pattern = pattern[0]
    frame_count = source.shape[0]
    model_width = source.shape[1]
    head_width = projections.shape[2]
    local_blocks = frame_count // BLK
    cycle_size = lax.axis_size("tm")
    nblocks = local_blocks * cycle_size
    first_block = lax.axis_index("tm") * local_blocks
    half_width = KW // 2
    contract = (((0,), (0,)), ((), ()))
    listed, live_mask = key_lists(rows_pattern, first_block, nblocks)
    queries = jnp.dot(source, projections[0], preferred_element_type=jnp.float32).astype(
        jnp.bfloat16
    )
    key_rows = jnp.dot(source, projections[1], preferred_element_type=jnp.float32).astype(
        jnp.bfloat16
    )
    values = jnp.dot(source, projections[2], preferred_element_type=jnp.float32).astype(
        jnp.bfloat16
    )
    key_all, value_all = (
        lax.all_gather(key_rows, "tm", axis=0, tiled=True),
        lax.all_gather(values, "tm", axis=0, tiled=True),
    )
    mixed_rows, logsum = attend(queries, key_all, value_all, listed, live_mask, BLK, HD)
    output_part = lax.dot_general(
        mixed_rows, projections[3], (((1,), (1,)), ((), ())), preferred_element_type=jnp.float32
    )
    summed = lax.psum(output_part.astype(jnp.bfloat16), "head").astype(jnp.float32)
    residual = (source.astype(jnp.float32) + summed).astype(jnp.bfloat16)
    extended = extended_2(jnp.concatenate([residual, upstream], axis=1), (("tm", 0),), half_width)
    encoded, back_grad, kernel_grad = conv_apply(
        residual, upstream, extended, kernel, frame_count, model_width, half_width
    )
    grad_mixed = jnp.dot(back_grad, projections[3], preferred_element_type=jnp.float32).astype(
        jnp.bfloat16
    )
    grad_queries, _, key_grad, value_grad = attend_back(
        queries,
        key_all,
        value_all,
        listed,
        live_mask,
        logsum,
        mixed_rows,
        grad_mixed,
        BLK,
        HD,
        nblocks,
    )
    key_value_terms = jnp.concatenate([key_grad, value_grad], axis=1)
    owned = lax.psum_scatter(
        key_value_terms.astype(jnp.bfloat16), "tm", scatter_dimension=0, tiled=True
    ).astype(jnp.float32)
    key_own = owned[:, :head_width].astype(jnp.bfloat16)
    value_own = owned[:, head_width:].astype(jnp.bfloat16)
    proj_grad = jnp.stack(
        [
            lax.dot_general(source, grad_queries, contract, preferred_element_type=jnp.float32),
            lax.dot_general(source, key_own, contract, preferred_element_type=jnp.float32),
            lax.dot_general(source, value_own, contract, preferred_element_type=jnp.float32),
            lax.dot_general(back_grad, mixed_rows, contract, preferred_element_type=jnp.float32),
        ]
    )
    proj_result, kernel_result = (
        lax.psum_scatter(
            proj_grad.astype(jnp.bfloat16), ("dp", "tm"), scatter_dimension=1, tiled=True
        ).astype(jnp.float32),
        lax.psum_scatter(
            kernel_grad.astype(jnp.bfloat16), ("dp", "tm"), scatter_dimension=0, tiled=True
        ).astype(jnp.float32),
    )
    return (encoded[None], proj_result, kernel_result)


NN = (((1,), (0,)), ((), ()))
NT = (((1,), (1,)), ((), ()))
TN = (((0,), (0,)), ((), ()))


def dot32(left, right, dims):
    return lax.dot_general(left, right, dims, preferred_element_type=jnp.float32)


def biased_scores(keys, query, bias):
    blocks, count = bias.shape
    wide = jnp.broadcast_to(bias[:, None, :], (blocks, BLK, count)).reshape(blocks * BLK, count)
    return dot32(keys, query, NT) * HD ** (-0.5) + wide


def head_slices(width, head):
    return [slice(i * width + head * HD, i * width + (head + 1) * HD) for i in range(3)]


def forward_kernel(bias_ref, qkv_own, qkv_far, mixed_own, mixed_far, logsum_ref):
    half, width = mixed_own.shape
    for head in range(width // HD):
        cols, kcols, vcols = head_slices(width, head)
        keys = jnp.concatenate([qkv_own[:, kcols], qkv_far[:, kcols]], axis=0)
        vals = jnp.concatenate([qkv_own[:, vcols], qkv_far[:, vcols]], axis=0)
        for part, (qkv, mixed_out) in enumerate(((qkv_own, mixed_own), (qkv_far, mixed_far))):
            span = slice(part * half, (part + 1) * half)
            scores = biased_scores(keys, qkv[:, cols], bias_ref[:, span])
            highest = jnp.max(scores, axis=0, keepdims=True)
            powers = jnp.exp(scores - highest)
            total = jnp.sum(powers, axis=0, keepdims=True)
            weights = (powers * (1.0 / total)).astype(jnp.bfloat16)
            mixed_out[:, cols] = dot32(vals, weights, TN).T.astype(jnp.bfloat16)
            logsum_ref[head : head + 1, span] = highest + jnp.log(total)


def backward_kernel(
    bias_ref, logsum_ref, qkv_own, qkv_far, grad_own, grad_far, mixed_own, mixed_far, terms_own, terms_far
):
    half, width = mixed_own.shape
    bf16, f32 = (jnp.bfloat16, jnp.float32)
    sides = ((qkv_own, grad_own, mixed_own, terms_own), (qkv_far, grad_far, mixed_far, terms_far))
    for head in range(width // HD):
        cols, kcols, vcols = head_slices(width, head)
        keys = jnp.concatenate([qkv_own[:, kcols], qkv_far[:, kcols]], axis=0)
        vals = jnp.concatenate([qkv_own[:, vcols], qkv_far[:, vcols]], axis=0)
        key_grad = jnp.zeros((2 * half, HD), f32)
        value_grad = jnp.zeros((2 * half, HD), f32)
        for part, (qkv, grads, mixed, terms) in enumerate(sides):
            span = slice(part * half, (part + 1) * half)
            query, grad = (qkv[:, cols], grads[:, cols])
            scores = biased_scores(keys, query, bias_ref[:, span])
            prob = jnp.exp(scores - logsum_ref[head : head + 1, span])
            weights = prob.astype(bf16)
            product = grad.astype(f32) * mixed[:, cols].astype(f32)
            delta = jnp.sum(product.T, axis=0, keepdims=True)
            grad_prob = dot32(vals, grad, NT)
            grad_scores = (prob * (grad_prob - delta) * HD ** (-0.5)).astype(bf16)
            terms[:, cols] = dot32(keys, grad_scores, TN).T.astype(bf16)
            key_grad = key_grad + dot32(grad_scores, query, NN)
            value_grad = value_grad + dot32(weights, grad, NN)
        for part, terms in enumerate((terms_own, terms_far)):
            rows = slice(part * half, (part + 1) * half)
            terms[:, kcols] = key_grad[rows].astype(bf16)
            terms[:, vcols] = value_grad[rows].astype(bf16)


def attend_forward(bias, qkv_own, qkv_far):
    half, width = (qkv_own.shape[0], qkv_own.shape[1] // 3)
    mixed = jax.ShapeDtypeStruct((half, width), jnp.bfloat16)
    pairs = (2 * half) ** 2 * (width // HD)
    return pl.pallas_call(
        forward_kernel,
        out_shape=(mixed, mixed, jax.ShapeDtypeStruct((8, 2 * half), jnp.float32)),
        compiler_params=pltpu.CompilerParams(vmem_limit_bytes=40 << 20),
        cost_estimate=pl.CostEstimate(
            flops=4 * pairs * HD, bytes_accessed=8 * half * width * 2, transcendentals=pairs
        ),
        name="attnfwd",
    )(bias, qkv_own, qkv_far)


def attend_backward(bias, logsum, qkv_own, qkv_far, grad_own, grad_far, mixed_own, mixed_far):
    half, width = grad_own.shape
    terms = jax.ShapeDtypeStruct((half, 3 * width), jnp.bfloat16)
    pairs = (2 * half) ** 2 * (width // HD)
    return pl.pallas_call(
        backward_kernel,
        out_shape=(terms, terms),
        compiler_params=pltpu.CompilerParams(vmem_limit_bytes=40 << 20),
        cost_estimate=pl.CostEstimate(
            flops=10 * pairs * HD, bytes_accessed=16 * half * width * 2, transcendentals=pairs
        ),
        name="attnbwd",
    )(bias, logsum, qkv_own, qkv_far, grad_own, grad_far, mixed_own, mixed_far)


LANES = 128


def conv_rows(rows):
    return next(size for size in (64, 48, 32, 16) if rows % size == 0)


def fill_padded(padded, rows, halo, flag_ref):
    half_width = KW // 2
    count = rows.shape[0]
    upper = flag_ref[0, 0] == 1
    padded[0:half_width] = jnp.where(upper, halo, 0.0)
    padded[half_width : half_width + count] = rows
    padded[half_width + count : 2 * half_width + count] = jnp.where(upper, 0.0, halo)


def back_conv_kernel(flag_ref, up_ref, halo_ref, taps_ref, out_ref, padded):
    count = up_ref.shape[0]
    step = conv_rows(count)
    for chunk in range(up_ref.shape[1] // LANES):
        cols = slice(chunk * LANES, (chunk + 1) * LANES)
        rows = up_ref[:, cols].astype(jnp.float32)
        fill_padded(padded, rows, halo_ref[:, cols].astype(jnp.float32), flag_ref)
        taps = taps_ref[:, cols].astype(jnp.float32)

        def body(tile, carry, cols=cols, taps=taps):
            start = pl.multiple_of(tile * step, step)
            total = padded[pl.ds(start + KW // 2, step)]
            for offset in range(KW):
                total = total + taps[offset : offset + 1] * padded[pl.ds(start + KW - offset, step)]
            out_ref[pl.ds(start, step), cols] = total.astype(jnp.bfloat16)
            return carry

        lax.fori_loop(0, count // step, body, 0)


def back_conv(flag, upstream, halo, taps):
    count, width = upstream.shape
    return pl.pallas_call(
        back_conv_kernel,
        out_shape=jax.ShapeDtypeStruct((count, width), jnp.bfloat16),
        in_specs=[pl.BlockSpec(memory_space=pltpu.SMEM)] + [pl.BlockSpec(memory_space=pltpu.VMEM)] * 3,
        scratch_shapes=[pltpu.VMEM((count + KW + 8, LANES), jnp.float32)],
        cost_estimate=pl.CostEstimate(flops=2 * KW * count * width * 40, bytes_accessed=4 * count * width, transcendentals=0),
        name="back_conv",
    )(flag, upstream, halo, taps)


def conv_kernel(flag_ref, rows_ref, up_ref, taps_ref, out_ref, grad_ref, padded, sums):
    count = up_ref.shape[0]
    step = conv_rows(count)
    for chunk in range(rows_ref.shape[1] // LANES):
        cols = slice(chunk * LANES, (chunk + 1) * LANES)
        rows = rows_ref[:, cols].astype(jnp.float32)
        fill_padded(padded, rows[:count], rows[count:], flag_ref)
        taps = taps_ref[:, cols].astype(jnp.float32)
        sums[...] = jnp.zeros_like(sums)

        def body(tile, carry, cols=cols, taps=taps):
            start = pl.multiple_of(tile * step, step)
            total = padded[pl.ds(start + KW // 2, step)]
            upstream = up_ref[pl.ds(start, step), cols].astype(jnp.float32)
            for offset in range(KW):
                shifted = padded[pl.ds(start + offset, step)]
                total = total + taps[offset : offset + 1] * shifted
                product = (upstream * shifted).reshape(step // 8, 8, LANES)
                sums[offset] = sums[offset] + jnp.sum(product, axis=0)
            out_ref[pl.ds(start, step), cols] = total.astype(jnp.bfloat16)
            return carry

        lax.fori_loop(0, count // step, body, 0)
        grad_ref[:, cols] = jnp.sum(sums[...], axis=1)


def conv(flag, rows, upstream, taps):
    count, width = upstream.shape
    return pl.pallas_call(
        conv_kernel,
        out_shape=(
            jax.ShapeDtypeStruct((count, width), jnp.bfloat16),
            jax.ShapeDtypeStruct((KW, width), jnp.float32),
        ),
        in_specs=[pl.BlockSpec(memory_space=pltpu.SMEM)] + [pl.BlockSpec(memory_space=pltpu.VMEM)] * 3,
        scratch_shapes=[
            pltpu.VMEM((count + KW + 8, LANES), jnp.float32),
            pltpu.VMEM((KW, 8, LANES), jnp.float32),
        ],
        cost_estimate=pl.CostEstimate(flops=4 * KW * count * width * 40, bytes_accessed=6 * count * width, transcendentals=0),
        name="conv",
    )(flag, rows, upstream, taps)


SIDE = [(0, 1), (1, 0)]
CORE = [(0, 1), (1, 0), (2, 3), (3, 2)]
CHIP = [(0, 2), (2, 0), (1, 3), (3, 1)]
CROSS = [(0, 3), (3, 0), (1, 2), (2, 1)]


def columns(array, index, width):
    return lax.dynamic_slice_in_dim(array, index * width, width, axis=1)


def live_bias(pattern, far_pattern, side, local):
    order = jnp.concatenate(
        [side * local + jnp.arange(local), (1 - side) * local + jnp.arange(local)]
    ).astype(jnp.int32)
    chosen = jnp.concatenate([pattern, far_pattern], axis=0)
    near = jnp.abs(order[:, None] - order[None, :]) <= 1
    listed = jnp.any(chosen[None, :, :] == order[:, None, None], axis=-1)
    bias = jnp.where(near | listed, 0.0, -1e30).astype(jnp.float32)
    return jnp.repeat(bias, BLK, axis=1)


def split_heads(frames, projections, kernel, pattern, cotangent):
    return split_heads_body(frames[0], projections, kernel, pattern[0], cotangent[0])


def split_heads_body(source, projections, kernel, pattern, upstream):
    bf16, f32 = (jnp.bfloat16, jnp.float32)
    count, width = source.shape
    local = count // BLK
    half_width = KW // 2
    ring_size = lax.axis_size("dp")
    head_width = projections.shape[2]
    mine_width = head_width // 2
    quarter = width // 4
    shard = width // ring_size
    side, head, place = (lax.axis_index("tm"), lax.axis_index("head"), lax.axis_index("dp"))
    first = side == 0
    flag = side.astype(jnp.int32).reshape(1, 1)

    def pick(array):
        low, high = (array[:, :mine_width], array[:, mine_width:])
        return (jnp.where(first, low, high), jnp.where(first, high, low))

    def edge(array):
        return jnp.where(first, array[count - half_width :], array[:half_width])

    def far_edge(array):
        return jnp.where(first, array[:half_width], array[count - half_width :])

    payload = jnp.concatenate(
        [
            edge(upstream),
            jnp.pad(
                pattern.astype(bf16),
                ((0, half_width - local), (0, LANES - pattern.shape[1])),
                constant_values=-1,
            ),
        ],
        axis=1,
    )
    arrived = lax.ppermute(payload, "tm", SIDE)
    up_halo = arrived[:, :width]
    far_pattern = arrived[:local, width : width + pattern.shape[1]].astype(jnp.int32)
    frames_mine = columns(source, head, quarter)
    far_mine = lax.ppermute(frames_mine, "tm", SIDE)

    def project(rows, index):
        whole = jnp.dot(rows, projections[index], preferred_element_type=f32).astype(bf16)
        return pick(whole)

    query_keep, query_send = project(source, 0)
    gated, _ = lax.optimization_barrier((source, arrived))
    key_keep, key_send = project(gated, 1)
    value_keep, value_send = project(gated, 2)
    qkv_own = jnp.concatenate([query_keep, key_keep, value_keep], axis=1)
    qkv_send = jnp.concatenate([query_send, key_send, value_send], axis=1)
    qkv_far = lax.ppermute(qkv_send, "tm", SIDE)
    bias = live_bias(pattern, far_pattern, side, local)

    far_across = lax.ppermute(far_mine, "head", CORE)
    far_beside = lax.ppermute(far_mine, "head", CHIP)
    far_corner = lax.ppermute(far_beside, "head", CORE)
    far_frames = jnp.stack([far_mine, far_across, far_beside, far_corner])
    back_grad = back_conv(flag, upstream, up_halo, kernel)
    grad_mixed = jnp.dot(back_grad, projections[3], preferred_element_type=f32).astype(bf16)
    grad_own, grad_send = pick(grad_mixed)
    grad_far = lax.ppermute(grad_send, "tm", SIDE)

    mixed_own, mixed_far, logsum = attend_forward(bias, qkv_own, qkv_far)
    mixed_got = lax.ppermute(jnp.concatenate([mixed_far, edge(mixed_own)], axis=0), "tm", SIDE)
    terms_own, terms_far = attend_backward(
        bias, logsum, qkv_own, qkv_far, grad_own, grad_far, mixed_own, mixed_far
    )

    onward = [(i, (i + 1) % ring_size) for i in range(ring_size)]
    rows = shard // 2

    def chunk_index(step):
        return (place + (2 * ring_size - 1 - step)) % ring_size

    def halves(array):
        return (
            jnp.where(first, array[rows:], array[:rows]),
            jnp.where(first, array[:rows], array[rows:]),
        )

    def attention_chunk(step, own, far):
        index = chunk_index(step)
        far_f = lax.dynamic_index_in_dim(far_frames, index ^ head, 0, keepdims=False)
        near_f = columns(source, index, shard)
        return dot32(near_f, own, TN) + dot32(far_f, far, TN)

    away, home = [part.astype(bf16) for part in halves(attention_chunk(0, terms_own, terms_far))]
    for step in range(1, ring_size):
        away_got = lax.ppermute(away, "dp", onward)
        home_got = lax.ppermute(home, "dp", onward)
        own, far, _ = lax.optimization_barrier((terms_own, terms_far, away))
        away_term, home_term = halves(attention_chunk(step, own, far))
        away = (away_term + away_got.astype(f32)).astype(bf16)
        home_got, _ = lax.optimization_barrier((home_got, away))
        home = (home_term + home_got.astype(f32)).astype(bf16)
    swap_got = lax.ppermute(away, "tm", SIDE)

    mixed_left = jnp.concatenate([mixed_own, far_edge(mixed_far)], axis=0)
    mixed_rows = jnp.concatenate(
        [jnp.where(first, mixed_left, mixed_got), jnp.where(first, mixed_got, mixed_left)], axis=1
    )
    out_grad = dot32(back_grad, mixed_rows[:count], TN)
    out_grad = out_grad.reshape(ring_size, 2, rows, head_width)
    out_send = jnp.where(first, out_grad[:, 1], out_grad[:, 0]).astype(bf16)
    out_got = lax.ppermute(out_send, "tm", SIDE)
    out_sum = jnp.where(first, out_grad[:, 0], out_grad[:, 1]) + out_got.astype(f32)
    out_chunk = lax.dynamic_index_in_dim(out_sum, chunk_index(0), 0, keepdims=False).astype(bf16)
    for step in range(1, ring_size):
        out_arrived = lax.ppermute(out_chunk, "dp", onward)
        term = lax.dynamic_index_in_dim(out_sum, chunk_index(step), 0, keepdims=False)
        out_chunk = (term + out_arrived.astype(f32)).astype(bf16)

    output_part = dot32(mixed_rows, projections[3], NT).astype(bf16)
    low_core = head % 2 == 0
    low_chip = head // 2 == 0
    parts = [output_part[:, i * quarter : (i + 1) * quarter] for i in range(4)]
    core_keep = [jnp.where(low_core, parts[2 * i], parts[2 * i + 1]) for i in range(2)]
    core_send = jnp.stack([jnp.where(low_core, parts[2 * i + 1], parts[2 * i]) for i in range(2)])
    core_got = lax.ppermute(core_send, "head", CORE)
    chip_sum = [core_keep[i].astype(f32) + core_got[i].astype(f32) for i in range(2)]
    chip_send = jnp.where(low_chip, chip_sum[1], chip_sum[0]).astype(bf16)
    chip_got = lax.ppermute(chip_send, "head", CHIP)
    summed = jnp.where(low_chip, chip_sum[0], chip_sum[1]) + chip_got.astype(f32)
    frames_rows = jnp.concatenate([frames_mine, far_edge(far_mine)], axis=0)
    residual = (frames_rows.astype(f32) + summed).astype(bf16)
    encoded, taps_grad = conv(
        flag, residual, columns(upstream, head, quarter), columns(kernel, head, quarter)
    )

    tap_rows = KW // (2 * ring_size)
    grouped = taps_grad.reshape(ring_size, 2, tap_rows, quarter)
    tap_keep = jnp.where(first, grouped[:, 0], grouped[:, 1])
    tap_send = jnp.where(first, grouped[:, 1], grouped[:, 0])
    tap_sum = tap_keep + lax.ppermute(tap_send, "tm", SIDE)
    tap_total = lax.dynamic_index_in_dim(tap_sum, place, 0, keepdims=False)
    for hop in range(1, ring_size):
        target = (place + hop) % ring_size
        leaving = lax.dynamic_index_in_dim(tap_sum, target, 0, keepdims=False)
        pairs = [(i, (i + hop) % ring_size) for i in range(ring_size)]
        tap_total = tap_total + lax.ppermute(leaving, "dp", pairs)

    def ordered(pieces):
        return jnp.concatenate(
            [lax.select_n((head ^ i).astype(jnp.int32), *pieces) for i in range(4)], axis=1
        )

    kernel_result = ordered(
        [tap_total]
        + [lax.ppermute(tap_total, "head", p) for p in (CORE, CHIP, CROSS)]
    )
    across = lax.ppermute(encoded, "head", CORE)
    beside = lax.ppermute(encoded, "head", CHIP)
    corner = lax.ppermute(beside, "head", CORE)
    encoded_all = ordered([encoded, across, beside, corner])

    left = jnp.where(first, home, swap_got)
    right = jnp.where(first, swap_got, home)
    proj_result = jnp.stack(
        [
            jnp.concatenate(
                [x[:, i * mine_width : (i + 1) * mine_width] for x in (left, right)], axis=1
            )
            for i in range(3)
        ]
        + [out_chunk]
    ).astype(f32)
    return (encoded_all[None], proj_result, kernel_result)


def solution(mesh):
    placed = (
        P("dp", "tm", None),
        P(None, None, "head"),
        P(),
        P("dp", "tm", None),
        P("dp", "tm", None),
    )
    sizes = dict(mesh.shape)
    small = sizes["tm"] == 2 and sizes["head"] == 4 and sizes["dp"] == 4

    def chosen(frames, projections, kernel, pattern, cotangent):
        fits = (
            small
            and frames.shape[1] <= 768
            and projections.shape[2] // 4 == 4 * HD
            and frames.shape[2] % (4 * LANES) == 0
        )
        return jax.shard_map(
            split_heads if fits else shards,
            mesh=mesh,
            in_specs=placed,
            out_specs=(P("dp", "tm", None), P(None, ("dp", "tm"), "head"), P(("dp", "tm"), None)),
            check_vma=False,
        )(frames, projections, kernel, pattern, cotangent)

    return chosen
```

```python
import functools

import jax
import jax.numpy as jnp
from jax import lax
from jax.experimental import pallas as pl
from jax.experimental.pallas import tpu as pltpu
from jax.sharding import PartitionSpec as P


HD = 96
BLK = 64
KW = 32


def extended_2(array, sides, width):
    for axis, dim in sides:
        peers, length = (lax.axis_size(axis), array.shape[dim])
        up = [(i, (i + 1) % peers) for i in range(peers - 1)]
        down = [(j, i) for i, j in up]
        last = lax.slice_in_dim(array, length - width, length, axis=dim)
        first = lax.slice_in_dim(array, 0, width, axis=dim)
        before = lax.ppermute(last, axis, up)
        after = lax.ppermute(first, axis, down)
        array = jnp.concatenate([before, array, after], axis=dim)
    return array


def key_lists(pattern, first_block, nblocks):
    query_count = pattern.shape[0]
    query_block = first_block + jnp.arange(query_count, dtype=jnp.int32)
    band_blocks = query_block[:, None] + jnp.arange(-1, 2, dtype=jnp.int32)[None, :]
    band_live = (band_blocks >= 0) & (band_blocks < nblocks)
    far_live = (pattern >= 0) & (jnp.abs(pattern - query_block[:, None]) > 1)
    listed = jnp.clip(jnp.concatenate([band_blocks, pattern], axis=1), 0, nblocks - 1)
    live_mask = jnp.concatenate([band_live, far_live], axis=1)
    return (listed, live_mask)


def gather_blocks(source, listed, block_len, head_dim):
    head_count = source.shape[1] // head_dim
    gathered = source.reshape(-1, block_len, head_count, head_dim)[listed]
    return gathered.reshape(listed.shape[0], listed.shape[1] * block_len, head_count, head_dim)


def masked_scores(query_tiles, key_tiles, live_mask, block_len):
    score_scale = query_tiles.shape[-1] ** (-0.5)
    scores = (
        jnp.einsum("qthd,qkhd->qhtk", query_tiles, key_tiles, preferred_element_type=jnp.float32)
        * score_scale
    )
    column_live = jnp.repeat(live_mask, block_len, axis=1)[:, None, None, :]
    return (jnp.where(column_live, scores, -1e30), column_live)


def attend(queries, key_rows, values, listed, live_mask, block_len, head_dim):
    head_count = queries.shape[1] // head_dim
    query_tiles = queries.reshape(listed.shape[0], block_len, head_count, head_dim)
    key_tiles = gather_blocks(key_rows, listed, block_len, head_dim)
    value_tiles = gather_blocks(values, listed, block_len, head_dim)
    scores, column_live = masked_scores(query_tiles, key_tiles, live_mask, block_len)
    highest = jnp.max(scores, axis=-1, keepdims=True)
    logsum = highest + jnp.log(jnp.sum(jnp.exp(scores - highest), axis=-1, keepdims=True))
    weights = jnp.where(column_live, jnp.exp(scores - logsum), 0.0).astype(jnp.bfloat16)
    mixed_rows = jnp.einsum(
        "qhtk,qkhd->qthd", weights, value_tiles, preferred_element_type=jnp.float32
    ).astype(jnp.bfloat16)
    return (mixed_rows.reshape(queries.shape), logsum)


def attend_back(
    queries,
    key_rows,
    values,
    listed,
    live_mask,
    logsum,
    mixed_rows,
    grad_mixed,
    block_len,
    head_dim,
    nblocks,
):
    head_count = queries.shape[1] // head_dim
    shape_tiles = (listed.shape[0], block_len, head_count, head_dim)
    query_tiles = queries.reshape(shape_tiles)
    grad_tiles = grad_mixed.reshape(shape_tiles)
    mixed_tiles = mixed_rows.reshape(shape_tiles)
    key_tiles = gather_blocks(key_rows, listed, block_len, head_dim)
    value_tiles = gather_blocks(values, listed, block_len, head_dim)
    scores, column_live = masked_scores(query_tiles, key_tiles, live_mask, block_len)
    probabilities = jnp.where(column_live, jnp.exp(scores - logsum), 0.0)
    row_delta = jnp.einsum(
        "qthd,qthd->qht", grad_tiles, mixed_tiles, preferred_element_type=jnp.float32
    )
    grad_probs = jnp.einsum(
        "qthd,qkhd->qhtk", grad_tiles, value_tiles, preferred_element_type=jnp.float32
    )
    score_scale = head_dim ** (-0.5)
    grad_scores = (probabilities * (grad_probs - row_delta[..., None]) * score_scale).astype(
        jnp.bfloat16
    )
    grad_queries = jnp.einsum(
        "qhtk,qkhd->qthd", grad_scores, key_tiles, preferred_element_type=jnp.float32
    )
    grad_queries = grad_queries.astype(jnp.bfloat16).reshape(queries.shape)
    weights = probabilities.astype(jnp.bfloat16)
    key_terms = jnp.einsum(
        "qhtk,qthd->qkhd", grad_scores, query_tiles, preferred_element_type=jnp.float32
    )
    value_terms = jnp.einsum(
        "qhtk,qthd->qkhd", weights, grad_tiles, preferred_element_type=jnp.float32
    )
    block_ids = jnp.arange(nblocks, dtype=jnp.int32)
    onehot = (
        (listed.reshape(-1)[:, None] == block_ids[None, :]) & live_mask.reshape(-1)[:, None]
    ).astype(jnp.float32)
    tile_width = block_len * queries.shape[1]
    key_grad = jnp.dot(onehot.T, key_terms.reshape(-1, tile_width), precision=lax.Precision.HIGHEST)
    value_grad = jnp.dot(
        onehot.T, value_terms.reshape(-1, tile_width), precision=lax.Precision.HIGHEST
    )
    key_grad = key_grad.reshape(nblocks * block_len, queries.shape[1])
    value_grad = value_grad.reshape(nblocks * block_len, queries.shape[1])
    return (grad_queries, row_delta, key_grad, value_grad)


def conv_apply(residual, upstream, extended, kernel_cols, frame_count, width, half_width):
    padded = extended[:, :width]
    padded_up = extended[:, width:]
    upstream_wide = upstream.astype(jnp.float32)
    encoded = residual.astype(jnp.float32)
    back_grad = upstream_wide
    taps_grad = []
    for offset in range(2 * half_width):
        weight_row = kernel_cols[offset].astype(jnp.float32)
        shifted = padded[offset : offset + frame_count].astype(jnp.float32)
        encoded = encoded + weight_row * shifted
        back_grad = back_grad + weight_row * padded_up[
            2 * half_width - offset : 2 * half_width - offset + frame_count
        ].astype(jnp.float32)
        taps_grad.append(jnp.sum(upstream_wide * shifted, axis=0))
    return (encoded.astype(jnp.bfloat16), back_grad.astype(jnp.bfloat16), jnp.stack(taps_grad))


def shards(frames, projections, kernel, pattern, cotangent):
    source = frames[0]
    upstream = cotangent[0]
    rows_pattern = pattern[0]
    frame_count = source.shape[0]
    model_width = source.shape[1]
    head_width = projections.shape[2]
    local_blocks = frame_count // BLK
    cycle_size = lax.axis_size("tm")
    nblocks = local_blocks * cycle_size
    first_block = lax.axis_index("tm") * local_blocks
    half_width = KW // 2
    contract = (((0,), (0,)), ((), ()))
    listed, live_mask = key_lists(rows_pattern, first_block, nblocks)
    queries = jnp.dot(source, projections[0], preferred_element_type=jnp.float32).astype(
        jnp.bfloat16
    )
    key_rows = jnp.dot(source, projections[1], preferred_element_type=jnp.float32).astype(
        jnp.bfloat16
    )
    values = jnp.dot(source, projections[2], preferred_element_type=jnp.float32).astype(
        jnp.bfloat16
    )
    key_all, value_all = (
        lax.all_gather(key_rows, "tm", axis=0, tiled=True),
        lax.all_gather(values, "tm", axis=0, tiled=True),
    )
    mixed_rows, logsum = attend(queries, key_all, value_all, listed, live_mask, BLK, HD)
    output_part = lax.dot_general(
        mixed_rows, projections[3], (((1,), (1,)), ((), ())), preferred_element_type=jnp.float32
    )
    summed = lax.psum(output_part.astype(jnp.bfloat16), "head").astype(jnp.float32)
    residual = (source.astype(jnp.float32) + summed).astype(jnp.bfloat16)
    extended = extended_2(jnp.concatenate([residual, upstream], axis=1), (("tm", 0),), half_width)
    encoded, back_grad, kernel_grad = conv_apply(
        residual, upstream, extended, kernel, frame_count, model_width, half_width
    )
    grad_mixed = jnp.dot(back_grad, projections[3], preferred_element_type=jnp.float32).astype(
        jnp.bfloat16
    )
    grad_queries, _, key_grad, value_grad = attend_back(
        queries,
        key_all,
        value_all,
        listed,
        live_mask,
        logsum,
        mixed_rows,
        grad_mixed,
        BLK,
        HD,
        nblocks,
    )
    key_value_terms = jnp.concatenate([key_grad, value_grad], axis=1)
    owned = lax.psum_scatter(
        key_value_terms.astype(jnp.bfloat16), "tm", scatter_dimension=0, tiled=True
    ).astype(jnp.float32)
    key_own = owned[:, :head_width].astype(jnp.bfloat16)
    value_own = owned[:, head_width:].astype(jnp.bfloat16)
    proj_grad = jnp.stack(
        [
            lax.dot_general(source, grad_queries, contract, preferred_element_type=jnp.float32),
            lax.dot_general(source, key_own, contract, preferred_element_type=jnp.float32),
            lax.dot_general(source, value_own, contract, preferred_element_type=jnp.float32),
            lax.dot_general(back_grad, mixed_rows, contract, preferred_element_type=jnp.float32),
        ]
    )
    proj_result, kernel_result = (
        lax.psum_scatter(
            proj_grad.astype(jnp.bfloat16), ("dp", "tm"), scatter_dimension=1, tiled=True
        ).astype(jnp.float32),
        lax.psum_scatter(
            kernel_grad.astype(jnp.bfloat16), ("dp", "tm"), scatter_dimension=0, tiled=True
        ).astype(jnp.float32),
    )
    return (encoded[None], proj_result, kernel_result)


NN = (((1,), (0,)), ((), ()))
NT = (((1,), (1,)), ((), ()))
TN = (((0,), (0,)), ((), ()))
LANES = 128
EDGE = KW // 2
BF16 = jnp.bfloat16
F32 = jnp.float32


def dot32(left, right, dims):
    return lax.dot_general(left, right, dims, preferred_element_type=F32)


def shape(*dims, dtype=BF16):
    return jax.ShapeDtypeStruct(dims, dtype)


def run(body, outs, flops, *args, **options):
    scalar = pl.BlockSpec(memory_space=pltpu.SMEM)
    whole = pl.BlockSpec(memory_space=pltpu.VMEM)
    options.setdefault("in_specs", [scalar] + [whole] * (len(args) - 1))
    moved = sum(int(x.size) * x.dtype.itemsize for x in args)
    return pl.pallas_call(
        body,
        out_shape=outs,
        compiler_params=pltpu.CompilerParams(vmem_limit_bytes=40 << 20),
        cost_estimate=pl.CostEstimate(flops=flops, bytes_accessed=moved, transcendentals=0),
        **options,
    )(*args)


def pack(array):
    rows = array.shape[0] // 2
    return jnp.concatenate([array[:rows], array[rows:]], axis=1)


def unpack(array):
    width = array.shape[1] // 2
    return jnp.concatenate([array[:, :width], array[:, width:]], axis=0)


def project_kernel(meta, source, weights, own_ref, send_ref):
    whole = dot32(source[...], weights[0], NN).astype(BF16)
    width = whole.shape[1] // 2
    low, high = (whole[:, :width], whole[:, width:])
    first = meta[0] == 0
    own_ref[0] = jnp.where(first, low, high)
    send_ref[0] = pack(jnp.where(first, high, low))


def project(meta, source, projections):
    count, width = source.shape
    cols = projections.shape[2]
    return run(
        project_kernel,
        (shape(3, count, cols // 2), shape(3, count // 2, cols)),
        6 * count * width * cols,
        meta,
        source,
        projections,
        grid=(3,),
        in_specs=[
            pl.BlockSpec(memory_space=pltpu.SMEM),
            pl.BlockSpec((count, width), lambda i: (0, 0)),
            pl.BlockSpec((1, width, cols), lambda i: (i, 0, 0)),
        ],
        out_specs=(
            pl.BlockSpec((1, count, cols // 2), lambda i: (i, 0, 0)),
            pl.BlockSpec((1, count // 2, cols), lambda i: (i, 0, 0)),
        ),
    )


def conv_rows(rows):
    return next(size for size in (64, 48, 32, 16) if rows % size == 0)


def fill_padded(padded, rows, halo, upper):
    count = rows.shape[0]
    padded[0:EDGE] = jnp.where(upper, halo, 0.0)
    padded[EDGE : EDGE + count] = rows
    padded[EDGE + count : 2 * EDGE + count] = jnp.where(upper, 0.0, halo)


def fill_taps(wide, taps):
    for offset in range(KW):
        wide[offset] = jnp.broadcast_to(taps[offset : offset + 1], (8, LANES))


def tapped(total, wide, offset, shifted):
    parts = (shifted.shape[0] // 8, 8, LANES)
    return total + (wide[offset][None] * shifted.reshape(parts)).reshape(shifted.shape)


def back_kernel(meta, up_ref, arrived, taps_ref, weights, back_ref, own_ref, send_ref, padded, wide, sums):
    count, width = up_ref.shape
    step = conv_rows(count)
    upper = meta[0] == 1
    for chunk in range(width // LANES):
        cols = slice(chunk * LANES, (chunk + 1) * LANES)
        rows = up_ref[:, cols].astype(F32)
        fill_padded(padded, rows, arrived[:, cols].astype(F32), upper)
        fill_taps(wide, taps_ref[:, cols].astype(F32))

        def body(tile, carry, cols=cols):
            start = pl.multiple_of(tile * step, step)
            total = padded[pl.ds(start + EDGE, step)]
            for phase in range(8):
                loaded = padded[pl.ds(start + phase + 1, step + KW - 8)]
                for block in range(KW // 8):
                    shifted = loaded[8 * block : 8 * block + step]
                    total = tapped(total, wide, KW - 1 - phase - 8 * block, shifted)
            back_ref[pl.ds(start, step), cols] = total.astype(BF16)
            return carry

        lax.fori_loop(0, count // step, body, 0)
        part = dot32(back_ref[:, cols], weights[0, cols, :], NN)
        sums[...] = part if chunk == 0 else sums[...] + part
    grad = sums[...].astype(BF16)
    half = grad.shape[1] // 2
    low, high = (grad[:, :half], grad[:, half:])
    own_ref[...] = jnp.where(upper, high, low)
    send_ref[...] = pack(jnp.where(upper, low, high))


def back_conv(meta, upstream, arrived, taps, projections):
    count, width = upstream.shape
    cols = projections.shape[2]
    whole = pl.BlockSpec(memory_space=pltpu.VMEM)
    return run(
        back_kernel,
        (shape(count, width), shape(count, cols // 2), shape(count // 2, cols)),
        2 * count * width * cols + 80 * KW * count * width,
        meta,
        upstream,
        arrived,
        taps,
        projections,
        grid=(1,),
        in_specs=[pl.BlockSpec(memory_space=pltpu.SMEM)]
        + [whole] * 3
        + [pl.BlockSpec((1, width, cols), lambda i: (3, 0, 0))],
        out_specs=(whole, whole, whole),
        scratch_shapes=[
            pltpu.VMEM((count + KW + 8, LANES), F32),
            pltpu.VMEM((KW, 8, LANES), F32),
            pltpu.VMEM((count, cols), F32),
        ],
    )


def head_parts(own, far, head):
    width = own.shape[2]
    cols = slice(head * HD, (head + 1) * HD)
    late = slice(width + head * HD, width + (head + 1) * HD)
    return [
        (own[i, :, cols], jnp.concatenate([far[i, :, cols], far[i, :, late]], axis=0))
        for i in range(own.shape[0])
    ]


def biased_scores(keys, query, bias):
    blocks, count = bias.shape
    wide = jnp.broadcast_to(bias[:, None, :], (blocks, BLK, count)).reshape(blocks * BLK, count)
    return dot32(keys, query, NT) * HD ** (-0.5) + wide


def forward_kernel(meta, bias_ref, own, far, mixed_own, mixed_far, send_ref, logsum_ref):
    half, width = mixed_own.shape
    first = meta[0] == 0
    for head in range(width // HD):
        cols = slice(head * HD, (head + 1) * HD)
        queries, keys, vals = head_parts(own, far, head)
        keys = jnp.concatenate(keys, axis=0)
        vals = jnp.concatenate(vals, axis=0)
        for part, mixed_out in enumerate((mixed_own, mixed_far)):
            span = slice(part * half, (part + 1) * half)
            scores = biased_scores(keys, queries[part], bias_ref[:, span])
            highest = jnp.max(scores, axis=0, keepdims=True)
            powers = jnp.exp(scores - highest)
            total = jnp.sum(powers, axis=0, keepdims=True)
            weights = (powers * (1.0 / total)).astype(BF16)
            mixed_out[:, cols] = dot32(vals, weights, TN).T.astype(BF16)
            logsum_ref[head : head + 1, span] = highest + jnp.log(total)
    send_ref[: half // 2] = pack(mixed_far[...])
    edge = jnp.where(first, mixed_own[half - EDGE :], mixed_own[:EDGE])
    send_ref[half // 2 :] = jnp.concatenate([edge, edge], axis=1)


def backward_kernel(
    meta, bias_ref, logsum_ref, own, far, grad_own, grad_far, mixed_own, mixed_far, terms_own, terms_far
):
    half, width = mixed_own.shape
    for head in range(width // HD):
        cols = slice(head * HD, (head + 1) * HD)
        queries, keys, vals = head_parts(own, far, head)
        keys = jnp.concatenate(keys, axis=0)
        vals = jnp.concatenate(vals, axis=0)
        late = slice(width + head * HD, width + (head + 1) * HD)
        grads = (grad_own[:, cols], jnp.concatenate([grad_far[:, cols], grad_far[:, late]], axis=0))
        key_grad = jnp.zeros((2 * half, HD), F32)
        value_grad = jnp.zeros((2 * half, HD), F32)
        for part, (mixed, terms) in enumerate(((mixed_own, terms_own), (mixed_far, terms_far))):
            span = slice(part * half, (part + 1) * half)
            query, grad = (queries[part], grads[part])
            scores = biased_scores(keys, query, bias_ref[:, span])
            prob = jnp.exp(scores - logsum_ref[head : head + 1, span])
            weights = prob.astype(BF16)
            product = grad.astype(F32) * mixed[:, cols].astype(F32)
            delta = jnp.sum(product.T, axis=0, keepdims=True)
            grad_prob = dot32(vals, grad, NT)
            grad_scores = (prob * (grad_prob - delta) * HD ** (-0.5)).astype(BF16)
            terms[:, cols] = dot32(keys, grad_scores, TN).T.astype(BF16)
            key_grad = key_grad + dot32(grad_scores, query, NN)
            value_grad = value_grad + dot32(weights, grad, NN)
        for part, terms in enumerate((terms_own, terms_far)):
            rows = slice(part * half, (part + 1) * half)
            terms[:, width + head * HD : width + (head + 1) * HD] = key_grad[rows].astype(BF16)
            terms[:, 2 * width + head * HD : 2 * width + (head + 1) * HD] = value_grad[rows].astype(BF16)


def output_kernel(meta, mixed_own, mixed_far, got, weights, rows_ref, keep_ref, send_ref):
    half, width = mixed_own.shape
    first, low_core = (meta[0] == 0, meta[1] % 2 == 0)
    far = mixed_far[...]
    mine = jnp.concatenate(
        [mixed_own[...], jnp.where(first, far[:EDGE], far[half - EDGE :])], axis=0
    )
    theirs = jnp.concatenate([unpack(got[: half // 2]), got[half // 2 :, :width]], axis=0)
    rows = jnp.concatenate(
        [jnp.where(first, mine, theirs), jnp.where(first, theirs, mine)], axis=1
    )
    rows_ref[...] = rows
    quarter = keep_ref.shape[2]
    for chip in range(2):
        even, odd = [
            dot32(rows, weights[0, i * quarter : (i + 1) * quarter, :], NT).astype(BF16)
            for i in (2 * chip, 2 * chip + 1)
        ]
        keep_ref[chip] = jnp.where(low_core, even, odd)
        send_ref[chip] = jnp.where(low_core, odd, even)


def output_grad_kernel(meta, back_ref, rows_ref, keep_ref, send_ref):
    parts, rows = keep_ref.shape[:2]
    count = back_ref.shape[0]
    first = meta[0] == 0
    mixed = rows_ref[:count]
    for part in range(parts):
        cols = slice(part * 2 * rows, (part + 1) * 2 * rows)
        grad = dot32(back_ref[:, cols], mixed, TN).astype(BF16)
        keep_ref[part] = jnp.where(first, grad[:rows], grad[rows:])
        send_ref[part] = jnp.where(first, grad[rows:], grad[:rows])


def pack_terms(array):
    width = array.shape[1] * 2 // 3
    return jnp.concatenate([array[:, :width], pack(array[:, width:])], axis=0)


def unpack_terms(array, rows):
    return jnp.concatenate([array[:rows], unpack(array[rows:])], axis=1)


def terms_kernel(meta, source, mine, across, beside, corner, own, far, away_ref, home_ref, *, shard):
    first = meta[0] == 0
    rows = shard // 2
    grads = jnp.concatenate([own[...], far[...]], axis=0)
    for step in range(away_ref.shape[0]):
        start = pl.multiple_of(meta[2 + step] * shard, LANES)
        piece = meta[2 + step] ^ meta[1]
        near = source[:, pl.ds(start, shard)]
        low = jnp.where(piece == 0, mine[...], across[...])
        high = jnp.where(piece == 2, beside[...], corner[...])
        frames = jnp.concatenate([near, jnp.where(piece < 2, low, high)], axis=0)
        chunk = dot32(frames, grads, TN).astype(BF16)
        away_ref[step] = pack_terms(jnp.where(first, chunk[rows:], chunk[:rows]))
        home_ref[step] = pack_terms(jnp.where(first, chunk[:rows], chunk[rows:]))


def conv_kernel(
    meta, mine, far, keep, got, up_ref, taps_ref, out_ref, grad_ref, padded, wide, sums
):
    count, width = mine.shape
    step = conv_rows(count)
    upper = meta[0] == 1
    for chunk in range(width // LANES):
        cols = slice(chunk * LANES, (chunk + 1) * LANES)
        where = pl.ds(pl.multiple_of(meta[1] * width + chunk * LANES, LANES), LANES)
        edge = jnp.where(upper, far[count - EDGE :, cols], far[:EDGE, cols])
        frames = jnp.concatenate([mine[:, cols], edge], axis=0)
        total = frames.astype(F32) + keep[:, cols] + got[:, cols].astype(F32)
        rows = total.astype(BF16).astype(F32)
        fill_padded(padded, rows[:count], rows[count:], upper)
        fill_taps(wide, taps_ref[:, where].astype(F32))
        sums[...] = jnp.zeros_like(sums)

        def body(tile, carry, cols=cols, where=where):
            start = pl.multiple_of(tile * step, step)
            total = padded[pl.ds(start + EDGE, step)]
            upstream = up_ref[pl.ds(start, step), where].astype(F32)
            for phase in range(8):
                loaded = padded[pl.ds(start + phase, step + KW - 8)]
                for block in range(KW // 8):
                    offset = phase + 8 * block
                    shifted = loaded[8 * block : 8 * block + step]
                    total = tapped(total, wide, offset, shifted)
                    product = (upstream * shifted).reshape(step // 8, 8, LANES)
                    sums[offset] = sums[offset] + jnp.sum(product, axis=0)
            out_ref[pl.ds(start, step), cols] = total.astype(BF16)
            return carry

        lax.fori_loop(0, count // step, body, 0)
        grad_ref[:, cols] = jnp.sum(sums[...], axis=1)


def final_kernel(meta, home, got, last, out_ref):
    rows, width = (out_ref.shape[1], out_ref.shape[2] // 2)
    first = meta[0] == 0
    mine, theirs = [unpack_terms(x[...], rows) for x in (home, got)]
    left = jnp.where(first, mine, theirs).astype(F32)
    right = jnp.where(first, theirs, mine).astype(F32)
    for i in range(3):
        cols = slice(i * width, (i + 1) * width)
        out_ref[i] = jnp.concatenate([left[:, cols], right[:, cols]], axis=1)
    out_ref[3] = last[...].astype(F32)


def place_kernel(meta, mine, across, beside, corner, out_ref):
    width = mine.shape[1]
    for i, piece in enumerate((mine, across, beside, corner)):
        start = pl.multiple_of((meta[1] ^ i) * width, LANES)
        out_ref[:, pl.ds(start, width)] = piece[...]


SIDE = [(0, 1), (1, 0)]
CORE = [(0, 1), (1, 0), (2, 3), (3, 2)]
CHIP = [(0, 2), (2, 0), (1, 3), (3, 1)]
CROSS = [(0, 3), (3, 0), (1, 2), (2, 1)]


def columns(array, index, width):
    return lax.dynamic_slice_in_dim(array, index * width, width, axis=1)


def live_bias(pattern, far_pattern, side, local):
    order = jnp.concatenate(
        [side * local + jnp.arange(local), (1 - side) * local + jnp.arange(local)]
    ).astype(jnp.int32)
    chosen = jnp.concatenate([pattern, far_pattern], axis=0)
    near = jnp.abs(order[:, None] - order[None, :]) <= 1
    listed = jnp.any(chosen[None, :, :] == order[:, None, None], axis=-1)
    bias = jnp.where(near | listed, 0.0, -1e30).astype(jnp.float32)
    return jnp.repeat(bias, BLK, axis=1)


def split_heads(frames, projections, kernel, pattern, cotangent):
    return split_heads_body(frames[0], projections, kernel, pattern[0], cotangent[0])


def split_heads_body(source, projections, kernel, pattern, upstream):
    count, width = source.shape
    local = count // BLK
    ring = lax.axis_size("dp")
    head_width = projections.shape[2]
    mine_width = head_width // 2
    quarter = width // 4
    shard = width // ring
    rows = shard // 2
    side, head, place = (lax.axis_index("tm"), lax.axis_index("head"), lax.axis_index("dp"))
    first = side == 0

    def chunk_index(step):
        return (place + (2 * ring - 1 - step)) % ring

    order = [chunk_index(step) for step in range(ring)]
    meta = jnp.stack([side, head] + order).astype(jnp.int32)
    later = jnp.stack([side, head] + order[1:]).astype(jnp.int32)

    payload = jnp.concatenate(
        [
            jnp.where(first, upstream[count - EDGE :], upstream[:EDGE]),
            jnp.pad(
                pattern.astype(BF16),
                ((0, EDGE - local), (0, LANES - pattern.shape[1])),
                constant_values=-1,
            ),
        ],
        axis=1,
    )
    arrived = lax.ppermute(payload, "tm", SIDE)
    far_pattern = arrived[:local, width : width + pattern.shape[1]].astype(jnp.int32)
    frames_mine = columns(source, head, quarter)
    far_mine = lax.ppermute(frames_mine, "tm", SIDE)

    own, send = project(meta, source, projections)
    far = lax.ppermute(send, "tm", SIDE)
    bias = live_bias(pattern, far_pattern, side, local)

    far_across = lax.ppermute(far_mine, "head", CORE)
    far_beside = lax.ppermute(far_mine, "head", CHIP)
    far_corner = lax.ppermute(far_beside, "head", CORE)
    back_grad, grad_own, grad_send = back_conv(meta, upstream, arrived, kernel, projections)
    grad_far = lax.ppermute(grad_send, "tm", SIDE)

    pairs = (2 * count) ** 2 * (mine_width // HD)
    mixed_own, mixed_far, mixed_send, logsum = run(
        forward_kernel,
        (
            shape(count, mine_width),
            shape(count, mine_width),
            shape(count // 2 + EDGE, head_width),
            shape(8, 2 * count, dtype=F32),
        ),
        4 * pairs * HD,
        meta,
        bias,
        own,
        far,
    )
    mixed_got = lax.ppermute(mixed_send, "tm", SIDE)
    terms_own, terms_far = run(
        backward_kernel,
        (shape(count, 3 * mine_width), shape(count, 3 * mine_width)),
        10 * pairs * HD,
        meta,
        bias,
        logsum,
        own,
        far,
        grad_own,
        grad_far,
        mixed_own,
        mixed_far,
    )

    onward = [(i, (i + 1) % ring) for i in range(ring)]
    packed = rows * 3 // 2

    def ring_terms(numbers, steps):
        return run(
            functools.partial(terms_kernel, shard=shard),
            (shape(steps, packed, shard), shape(steps, packed, shard)),
            12 * steps * count * shard * mine_width,
            numbers,
            source,
            far_mine,
            far_across,
            far_beside,
            far_corner,
            terms_own,
            terms_far,
        )

    away, home = [x[0] for x in ring_terms(meta, 1)]
    away_terms, home_terms = ring_terms(later, ring - 1)
    for step in range(1, ring):
        away_got = lax.ppermute(away, "dp", onward)
        home_got = lax.ppermute(home, "dp", onward)
        away = (away_terms[step - 1].astype(F32) + away_got.astype(F32)).astype(BF16)
        home_got, _ = lax.optimization_barrier((home_got, away))
        home = (home_terms[step - 1].astype(F32) + home_got.astype(F32)).astype(BF16)
    swap_got = lax.ppermute(away, "tm", SIDE)

    whole = pl.BlockSpec(memory_space=pltpu.VMEM)
    mixed_rows, core_keep, core_send = run(
        output_kernel,
        (
            shape(count + EDGE, head_width),
            shape(2, count + EDGE, quarter),
            shape(2, count + EDGE, quarter),
        ),
        2 * count * width * head_width,
        meta,
        mixed_own,
        mixed_far,
        mixed_got,
        projections,
        grid=(1,),
        in_specs=[pl.BlockSpec(memory_space=pltpu.SMEM)]
        + [whole] * 3
        + [pl.BlockSpec((1, width, head_width), lambda i: (3, 0, 0))],
        out_specs=(whole, whole, whole),
    )
    core_got = lax.ppermute(core_send, "head", CORE)
    out_keep, out_send = run(
        output_grad_kernel,
        (shape(ring, rows, head_width), shape(ring, rows, head_width)),
        2 * count * width * head_width,
        meta,
        back_grad,
        mixed_rows,
    )
    out_got = lax.ppermute(out_send, "tm", SIDE)

    def out_term(step):
        kept, came = [
            lax.dynamic_index_in_dim(x, order[step], 0, keepdims=False).astype(F32)
            for x in (out_keep, out_got)
        ]
        return kept + came

    out_chunk = out_term(0).astype(BF16)
    for step in range(1, ring):
        out_arrived = lax.ppermute(out_chunk, "dp", onward)
        out_chunk = (out_term(step) + out_arrived.astype(F32)).astype(BF16)

    low_chip = head // 2 == 0
    sums = core_keep.astype(F32) + core_got.astype(F32)
    chip_keep = jnp.where(low_chip, sums[0], sums[1])
    chip_send = jnp.where(low_chip, sums[1], sums[0]).astype(BF16)
    chip_got = lax.ppermute(chip_send, "head", CHIP)
    encoded, taps_grad = run(
        conv_kernel,
        (shape(count, quarter), shape(KW, quarter, dtype=F32)),
        160 * KW * count * quarter,
        meta,
        frames_mine,
        far_mine,
        chip_keep,
        chip_got,
        upstream,
        kernel,
        scratch_shapes=[
            pltpu.VMEM((count + KW + 8, LANES), F32),
            pltpu.VMEM((KW, 8, LANES), F32),
            pltpu.VMEM((KW, 8, LANES), F32),
        ],
    )

    tap_rows = KW // (2 * ring)
    grouped = taps_grad.reshape(ring, 2, tap_rows, quarter)
    tap_keep = jnp.where(first, grouped[:, 0], grouped[:, 1])
    tap_send = jnp.where(first, grouped[:, 1], grouped[:, 0])
    tap_sum = tap_keep + lax.ppermute(tap_send, "tm", SIDE)
    tap_total = lax.dynamic_index_in_dim(tap_sum, place, 0, keepdims=False)
    for hop in range(1, ring):
        leaving = lax.dynamic_index_in_dim(tap_sum, (place + hop) % ring, 0, keepdims=False)
        tap_total = tap_total + lax.ppermute(
            leaving, "dp", [(i, (i + hop) % ring) for i in range(ring)]
        )
    pieces = [tap_total]
    for group in (CORE, CHIP, CROSS):
        pieces.append(lax.ppermute(tap_total, "head", group))
    kernel_result = jnp.concatenate(
        [lax.select_n((head ^ i).astype(jnp.int32), *pieces) for i in range(4)], axis=1
    )
    beside = lax.ppermute(encoded, "head", CHIP)
    across = lax.ppermute(encoded, "head", CORE)
    corner = lax.ppermute(beside, "head", CORE)
    encoded_all = run(place_kernel, shape(count, width), 0, meta, encoded, across, beside, corner)
    proj_result = run(
        final_kernel, shape(4, rows, head_width, dtype=F32), 0, meta, home, swap_got, out_chunk
    )
    return (encoded_all[None], proj_result, kernel_result)


def solution(mesh):
    placed = (
        P("dp", "tm", None),
        P(None, None, "head"),
        P(),
        P("dp", "tm", None),
        P("dp", "tm", None),
    )
    sizes = dict(mesh.shape)
    small = sizes["tm"] == 2 and sizes["head"] == 4 and sizes["dp"] == 4

    def chosen(frames, projections, kernel, pattern, cotangent):
        fits = (
            small
            and frames.shape[1] <= 768
            and projections.shape[2] // 4 == 4 * HD
            and frames.shape[2] % (4 * LANES) == 0
        )
        return jax.shard_map(
            split_heads if fits else shards,
            mesh=mesh,
            in_specs=placed,
            out_specs=(P("dp", "tm", None), P(None, ("dp", "tm"), "head"), P(("dp", "tm"), None)),
            check_vma=False,
        )(frames, projections, kernel, pattern, cotangent)

    return chosen
```
